32 devices in a mesh: blk: 8 (over y, x, core), chan: 4 (over z).
Axes of the slice: x: 2, y: 2, z: 4, core: 2. Of those that a mesh axis runs over, the one named last changes fastest.
Arguments:
- positions: float32 [3, 1024], P(None, 'blk'), may hold values from 0 to 48, as said below
- species: int32 [1024], P('blk'), may hold values from 0 to 1
- node_features: float32 [64, 1024], P('chan', 'blk'), may hold values from -6 to 6
- block_mask: int32 [8, 7], P('blk'), may hold values from 0 to 1, as said below
- radial_weight: float32 [8, 64], P(None, 'chan'), may hold values from -2 to 2
- species_embed: float32 [64, 2], P('chan'), may hold values from 0.25 to 1.75
- center_embed: float32 [64, 2], P('chan'), may hold values from 0.25 to 1.75
- mix_weight: float32 [3, 64, 64], replicated, may hold values from -0.75 to 0.75
Outputs:
- descriptors: float32 [3, 64, 1024], P(None, 'chan', 'blk')
The draws below stay inside these ranges and needn't reach their ends.
Inputs may be any that keep to these rules, and one draw needn't show every extreme that they name: `positions`: atom g lies in slab s = g // 128: its first coordinate in [s * 5 / 3, (s + 1) * 5 / 3), the other two in [0, 48). An arbitrary set of kept slab pairs, symmetric between the two slabs of a pair: block_mask[i, 3 + k] equals block_mask[(i + k) mod 8, 3 - k]; the middle column is 1.
All inputs are finite; a program needn't handle non-finite values.
Results may differ from the reference program's by a relative error of at most 0.0035.
Values sent between devices are 32-bit elements; how exact they have to be, the bound alone decides.
No kernel may reach another device: no remote copies, remote signals or barrier semaphores. Data moves between devices by JAX's collectives and lax.ppermute only.
A program may use at most 64 MiB of HBM per device.

```python
import math
import jax
import jax.numpy as jnp
from jax import lax

ATOM_DEV = 128
C = 64
NB = 8
HOPS = 3
NSPEC = 2
ATOMS = 1024
N_BLK = 8


slab_width = 5.0 / 3.0


cross_width = 48.0


def draw_positions(key, part):
    base = jax.random.fold_in(key, 11)
    first_key, second_key = jax.random.split(base)
    slab_of = (jnp.arange(ATOMS, dtype=jnp.int32) // ATOM_DEV).astype(jnp.float32)
    fraction = jax.random.uniform(first_key, (ATOMS,), jnp.float32)
    transverse = jax.random.uniform(second_key, (2, ATOMS), jnp.float32) * cross_width
    along = (slab_of + 0.999 * fraction) * slab_width
    return jnp.concatenate([along[None], transverse], axis=0).astype(jnp.float32)


def draw_block_mask(key, part):
    base = jax.random.fold_in(key, 23)
    random_ints = jax.random.randint(base, (N_BLK, HOPS), 0, 4)
    forward = (random_ints > 0).astype(jnp.int32)
    block_rows = jnp.arange(N_BLK, dtype=jnp.int32)
    backward = jnp.stack([forward[(block_rows - step) % N_BLK, step - 1] for step in range(1, HOPS + 1)], axis=1)
    backward_cols = backward[:, ::-1]
    return jnp.concatenate([backward_cols, jnp.ones((N_BLK, 1), jnp.int32), forward], axis=1)


def place_ends(values, rng, least, largest):
    longest = values.shape.index(max(values.shape))
    spots = []
    for shift in (0, 1):
        where = [jax.random.randint(jax.random.fold_in(rng, axis), (), 0, length) for axis, length in enumerate(values.shape)]
        where[longest] = (where[longest] + shift) % values.shape[longest]
        spots.append(tuple(where))
    return values.at[spots[0]].set(least).at[spots[1]].set(largest)


def levels(stream_key, shape, shards, least, high):
    factor_of, own = 1.0, jax.random.fold_in(stream_key, 6)
    for axis_at, shards_of in shards:
        steps = jnp.exp(jax.random.uniform(jax.random.fold_in(own, axis_at), (shards_of,), jnp.float32, least / len(shards), high / len(shards)))
        factor_of = factor_of * jnp.repeat(steps, shape[axis_at] // shards_of).reshape([-1 if axis == axis_at else 1 for axis in range(len(shape))])
    return factor_of


def scatter_about(stream_key, extent, spread, bound, shards=(), held_as=jnp.bfloat16):
    loudness = levels(stream_key, extent, shards, -0.22, 0.18) if shards else 1.0
    values = jax.random.normal(stream_key, extent, jnp.float32) * spread * loudness
    return jnp.minimum(jnp.maximum(values, -bound), bound).astype(held_as)


def setup_inputs(seed: int = 0) -> dict:
    keys = jax.random.split(jax.random.key(seed), 9)
    return {
        "positions": draw_positions(jax.random.fold_in(keys[8], 71), 0),
        "species": place_ends(jax.random.randint(keys[1], (ATOMS,), 0, NSPEC), jax.random.fold_in(keys[1], 1), 0, NSPEC - 1).astype(jnp.int32),
        "node_features": scatter_about(keys[2], (C, ATOMS), 1.0, 6.0, ((0, 4), (1, 8)), jnp.float32),
        "block_mask": draw_block_mask(jax.random.fold_in(keys[8], 71), 0),
        "radial_weight": scatter_about(keys[4], (NB, C), NB ** -0.5, 2.0, ((1, 4),), jnp.float32),
        "species_embed": jnp.clip(1.0 + 0.15 * jax.random.normal(keys[5], (C, NSPEC), jnp.float32), 0.25, 1.75),
        "center_embed": jnp.clip(1.0 + 0.15 * jax.random.normal(keys[6], (C, NSPEC), jnp.float32), 0.25, 1.75),
        "mix_weight": scatter_about(keys[7], (3, C, C), C ** -0.5, 0.75, (), jnp.float32),
    }


slab_width = 5.0 / 3.0
cross_width = 48.0
cut_radius = 5.0
soften = 0.25

def table_of(own_pos, other_pos, box_x, keep_pairs, count):
    separation = other_pos[:, None, :] - own_pos[:, :, None]
    lengths = jnp.array([box_x, cross_width, cross_width], dtype=jnp.float32)[:, None, None]
    separation = separation - lengths * jnp.floor(separation / lengths + 0.5)
    distance = jnp.sqrt(lax.optimization_barrier(jnp.sum(separation * separation, axis=0)) + soften)
    unit_x = separation[0] / distance
    unit_y = separation[1] / distance
    unit_z = separation[2] / distance
    root3 = math.sqrt(3.0)
    root15 = math.sqrt(15.0)
    harmonics = jnp.stack([jnp.ones_like(distance), root3 * unit_x, root3 * unit_y, root3 * unit_z, root15 * unit_x * unit_y, root15 * unit_y * unit_z, 0.5 * math.sqrt(5.0) * (2.0 * unit_z * unit_z - unit_x * unit_x - unit_y * unit_y), root15 * unit_x * unit_z, 0.5 * root15 * (unit_x * unit_x - unit_y * unit_y)])
    scaled = distance / cut_radius
    polynomial = 1.0 - 28.0 * scaled ** 6 + 48.0 * scaled ** 7 - 21.0 * scaled ** 8
    envelope = jnp.where(scaled < 1.0, polynomial, 0.0) * keep_pairs
    orders = jnp.arange(1, count + 1, dtype=jnp.float32)[:, None, None]
    radial = math.sqrt(2.0 / cut_radius) * jnp.sin(orders * (math.pi / cut_radius) * distance[None]) / distance[None] * envelope[None]
    return (radial[:, None] * harmonics[None]).astype(jnp.bfloat16)

def weights_lm(mix_weight):
    return jnp.concatenate([mix_weight[0:1], jnp.repeat(mix_weight[1:2], 3, axis=0), jnp.repeat(mix_weight[2:3], 5, axis=0)], axis=0)

def describe(mixed_tensor):
    squares = mixed_tensor * mixed_tensor
    return jnp.log1p(jnp.stack([squares[:, 0], lax.optimization_barrier(jnp.sum(squares[:, 1:4], axis=1)), lax.optimization_barrier(jnp.sum(squares[:, 4:9], axis=1))]))

def reference(positions, species, node_features, block_mask, radial_weight, species_embed, center_embed, mix_weight):
    box_x = float(N_BLK) * slab_width
    kinds = species_embed.shape[1]
    one_hot = (species[None, :] == jnp.arange(kinds, dtype=jnp.int32)[:, None]).astype(jnp.float32)
    embedded = jnp.dot(species_embed, one_hot, precision=lax.Precision.HIGHEST)
    centre = jnp.dot(center_embed, one_hot, precision=lax.Precision.HIGHEST)
    carried = (radial_weight[:, :, None] * (node_features * embedded)[None]).astype(jnp.bfloat16)
    pos_blocks = positions.reshape(3, N_BLK, ATOM_DEV).transpose(1, 0, 2)
    carried_blocks = carried.reshape(NB, C, N_BLK, ATOM_DEV).transpose(2, 0, 1, 3)
    no_self = 1.0 - jnp.eye(ATOM_DEV, dtype=jnp.float32)

    def one_block(block_id):
        own_pos = pos_blocks[block_id]
        summed = jnp.zeros((C, 9, ATOM_DEV), jnp.float32)
        for offset in range(-HOPS, HOPS + 1):
            neighbour = (block_id + offset) % N_BLK
            active = block_mask[block_id, HOPS + offset].astype(jnp.float32)
            keep_pairs = active * no_self if offset == 0 else active
            pair_table = table_of(own_pos, pos_blocks[neighbour], box_x, keep_pairs, NB)
            summed = summed + jnp.einsum('ncb,nmab->cma', carried_blocks[neighbour].astype(jnp.float32), pair_table.astype(jnp.float32), precision=lax.Precision.HIGHEST)
        return summed
    blocks = lax.map(one_block, jnp.arange(N_BLK, dtype=jnp.int32))
    features = blocks.transpose(1, 2, 0, 3).reshape(C, 9, ATOMS) * centre[:, None, :]
    mixed_tensor = jnp.einsum('mpc,cma->pma', weights_lm(mix_weight), features, precision=lax.Precision.HIGHEST)
    return describe(mixed_tensor)
```

```python
import math

import jax
import jax.numpy as jnp
from jax import lax
from jax.experimental import pallas as pl
from jax.experimental.pallas import tpu as pltpu
from jax.sharding import PartitionSpec as P

slab_width = 5.0 / 3.0
cross_width = 48.0
cut_radius = 5.0
soften = 0.25
components = 9
orders = ((0, 1), (1, 4), (4, 9))
lanes = 128
tile = 16

cos_terms = (
    -0.6056998671923182,
    -0.8837930130905377,
    0.5945743675766054,
    -0.11556393696983189,
    0.011100594647768918,
    -0.0006430391121701238,
    2.490485442655993e-05,
)
sinc_terms = (
    0.22505602342469963,
    -0.30281424022132397,
    0.08828480791644601,
    -0.011306965460218523,
    0.0008171987621448651,
    -3.805921488925154e-05,
    1.2352514278347018e-06,
)


def horner(terms, v):
    value = jnp.full_like(v, terms[-1])
    for term in terms[-2::-1]:
        value = value * v + term
    return value


def pair_rows(own, other, box_x, count, apart):
    shift = []
    for axis, length in enumerate((box_x, cross_width, cross_width)):
        r = other[axis] - own[axis]
        shift.append(r - length * jnp.floor(r * (1.0 / length) + 0.5))
    x, y, z = shift
    xx, yy, zz = x * x, y * y, z * z
    s = xx + yy + zz + soften
    inverse = lax.rsqrt(s)
    d = s * inverse
    scaled = d * (1.0 / cut_radius)
    square = s * (1.0 / cut_radius**2)
    sixth = square * square * square
    envelope = 1.0 + sixth * (scaled * 48.0 - 28.0 - 21.0 * square)
    keep = s < cut_radius**2
    if apart is not None:
        keep = jnp.logical_and(keep, apart)
    v = s * (2.0 / cut_radius**2) - 1.0
    first = jnp.where(keep, envelope * math.sqrt(2.0 / cut_radius), 0.0) * horner(sinc_terms, v)
    twice = 2.0 * horner(cos_terms, v)
    radial = [first, twice * first]
    while len(radial) < count:
        radial.append(twice * radial[-1] - radial[-2])
    root3, root15 = math.sqrt(3.0), math.sqrt(15.0)
    over = inverse * inverse
    s15 = root15 * over
    over3 = root3 * inverse
    harmonics = [
        None,
        x * over3,
        y * over3,
        z * over3,
        x * y * s15,
        y * z * s15,
        (2.0 * zz - xx - yy) * (0.5 * math.sqrt(5.0) * over),
        x * z * s15,
        (xx - yy) * (0.5 * s15),
    ]
    return [[r if h is None else r * h for h in harmonics] for r in radial[:count]]


def pair_kernel(slabs, data_count, own_slab, first, last, box_x, count, *refs):
    refs = list(refs)
    pos_ref, act_ref, par_ref = refs[:3]
    data = refs[3 : 3 + data_count]
    rest = refs[3 + data_count :]
    if not first:
        acc_ref = rest.pop(0)
    if last:
        mix_ref = rest.pop(0)
    out_ref, table_ref, weight_ref, sum_ref = rest
    channels = par_ref.shape[0]
    own = [jnp.broadcast_to(pos_ref[axis : axis + 1, :], (tile, lanes)) for axis in range(3)]
    for place, (which, base, index) in enumerate(slabs):
        ref = data[which]
        feats = ref[base : base + channels, :] * act_ref[index : index + 1, :]
        columns = ref[base + channels : base + channels + 8, :].T
        for n in range(count):
            weight_ref[:, n * lanes : (n + 1) * lanes] = (par_ref[:, n : n + 1] * feats).astype(
                jnp.bfloat16
            )
        for step in range(lanes // tile):
            rows = slice(step * tile, (step + 1) * tile)
            other = [
                jnp.broadcast_to(columns[rows, axis : axis + 1], (tile, lanes)) for axis in range(3)
            ]
            apart = None
            if index == own_slab:
                apart = (
                    lax.broadcasted_iota(jnp.int32, (tile, lanes), 0) + step * tile
                ) != lax.broadcasted_iota(jnp.int32, (tile, lanes), 1)
            table = pair_rows(own, other, box_x, count, apart)
            for n in range(count):
                for m in range(components):
                    table_ref[
                        n * lanes + step * tile : n * lanes + (step + 1) * tile,
                        m * lanes : (m + 1) * lanes,
                    ] = table[n][m].astype(jnp.bfloat16)
        part = jnp.dot(weight_ref[...], table_ref[...], preferred_element_type=jnp.float32)
        target = out_ref if not last else sum_ref
        if place == 0:
            target[...] = part if first else acc_ref[...] + part
        else:
            target[...] += part
    if not last:
        return
    kinds = par_ref.shape[1] - count
    centre = jnp.zeros((channels, lanes), jnp.float32)
    for kind in range(kinds):
        here = pos_ref[3:4, :] == float(kind)
        centre = jnp.where(here, par_ref[:, count + kind : count + kind + 1], centre)
    for order, (start, stop) in enumerate(orders):
        mix = mix_ref[order]
        mix_high = mix.astype(jnp.bfloat16)
        mix_low = (mix - mix_high.astype(jnp.float32)).astype(jnp.bfloat16)
        total = None
        for m in range(start, stop):
            features = sum_ref[:, m * lanes : (m + 1) * lanes] * centre
            high = features.astype(jnp.bfloat16)
            low = (features - high.astype(jnp.float32)).astype(jnp.bfloat16)
            mixed = (
                jnp.dot(mix_high, high, preferred_element_type=jnp.float32)
                + jnp.dot(mix_high, low, preferred_element_type=jnp.float32)
                + jnp.dot(mix_low, high, preferred_element_type=jnp.float32)
            )
            total = mixed * mixed if total is None else total + mixed * mixed
        out_ref[order] = jnp.log1p(total)


def accumulate(name, pos, act, par, data, slabs, own_slab, box_x, count, acc=None, mix=None):
    channels, atoms = par.shape[0], pos.shape[1]
    operands = [pos, act, par, *data]
    if acc is not None:
        operands.append(acc)
    if mix is not None:
        operands.append(mix)
    wide = (channels, components * atoms)
    shape = wide if mix is None else (mix.shape[0], mix.shape[1], atoms)
    flops = 2 * channels * count * components * atoms * atoms * len(slabs)

    def body(*refs):
        pair_kernel(
            slabs, len(data), own_slab, acc is None, mix is not None, box_x, count, *refs
        )

    return pl.pallas_call(
        body,
        out_shape=jax.ShapeDtypeStruct(shape, jnp.float32),
        in_specs=[pl.BlockSpec(memory_space=pltpu.VMEM)] * len(operands),
        out_specs=pl.BlockSpec(memory_space=pltpu.VMEM),
        scratch_shapes=[
            pltpu.VMEM((count * atoms, components * atoms), jnp.bfloat16),
            pltpu.VMEM((channels, count * atoms), jnp.bfloat16),
            pltpu.VMEM(wide if mix is not None else (8, lanes), jnp.float32),
        ],
        cost_estimate=pl.CostEstimate(flops=flops, bytes_accessed=1 << 20, transcendentals=0),
        name=name,
    )(*operands)


def moved(value, axis, target):
    size = lax.axis_size(axis)
    return lax.ppermute(value, axis, [(i, target(i, size)) for i in range(size)])


def flipped(value, axis, bit):
    return moved(value, axis, lambda i, size: i ^ bit)


def shards(
    positions,
    species,
    node_features,
    block_mask,
    radial_weight,
    species_embed,
    center_embed,
    mix_weight,
):
    slab_count = lax.axis_size("blk")
    owner_count = lax.axis_size("chan")
    box_x = float(slab_count) * slab_width
    reach = (block_mask.shape[1] - 1) // 2
    count = radial_weight.shape[0]
    kinds = species_embed.shape[1]
    held, atoms = node_features.shape
    me = lax.axis_index("blk")
    owner = lax.axis_index("chan")

    embedded = jnp.zeros((held, atoms), jnp.float32)
    for kind in range(kinds):
        embedded = jnp.where(species[None, :] == kind, species_embed[:, kind : kind + 1], embedded)
    rows = jnp.concatenate([radial_weight, center_embed.T], axis=0)
    rows = jnp.pad(rows, ((0, tile - count - kinds), (0, atoms - held)))
    owned = jnp.concatenate([node_features * embedded, rows], axis=0)[None]
    bit = owner_count // 2
    flips = [0]
    while bit:
        owned = jnp.concatenate([owned, flipped(owned, "chan", bit)], axis=0)
        flips = flips + [f ^ bit for f in flips]
        bit //= 2
    channels = held * owner_count
    feats = owned[:, :held].reshape(channels, atoms)
    par = owned[:, held : held + count + kinds, :held].transpose(0, 2, 1)
    par = par.reshape(channels, count + kinds)
    mine = lax.dynamic_slice_in_dim(mix_weight, owner * held, held, 1)
    mix = jnp.concatenate(
        [lax.dynamic_slice_in_dim(mine, (owner ^ f) * held, held, 2) for f in flips], axis=2
    )

    pos = jnp.concatenate(
        [positions, species[None].astype(jnp.float32), jnp.zeros((4, atoms), jnp.float32)], axis=0
    )
    bundle = jnp.concatenate([feats, pos], axis=0)
    depth = bundle.shape[0]

    def activity(places):
        offset = jnp.stack([lax.rem(p - me + reach + slab_count, slab_count) for p in places])
        at = offset[:, None] == jnp.arange(2 * reach + 1, dtype=jnp.int32)[None, :]
        value = jnp.sum(jnp.where(at, block_mask, 0), axis=1).astype(jnp.float32)
        return jnp.broadcast_to(value[:, None], (len(places), atoms))

    call = lambda name, act, data, slabs, acc=None, mix=None: accumulate(
        name, pos, act, par, data, slabs, 0, box_x, count, acc, mix
    )
    if slab_count == 2 * (reach + 1) == 8:
        act = activity([me ^ j for j in range(slab_count)])
        two = flipped(bundle, "blk", 2)
        pair = jnp.concatenate([bundle, two], axis=0)
        four = flipped(pair, "blk", 4)
        acc = call("near", act, [bundle, two], [(0, 0, 0), (1, 0, 2)])
        quad = jnp.concatenate([pair, four], axis=0)
        one = flipped(quad, "blk", 1)
        acc = call("middle", act, [four], [(0, depth, 6)], acc)
        return call("far", act, [one], [(0, j // 2 * depth, j) for j in (1, 3, 5, 7)], acc, mix)
    places = [0] + [k for h in range(1, reach + 1) for k in (h, -h)]
    act = activity([lax.rem(me + k + slab_count, slab_count) for k in places])
    act = jnp.pad(act, ((0, 8 - len(places)), (0, 0)))
    data = [bundle] + [
        moved(bundle, "blk", lambda i, size, k=k: (i - k) % size) for k in places[1:]
    ]
    return call("all", act, data, [(j, 0, j) for j in range(len(places))], None, mix)


def solution(mesh):
    return jax.shard_map(
        shards,
        mesh=mesh,
        in_specs=(
            P(None, "blk"),
            P("blk"),
            P("chan", "blk"),
            P("blk", None),
            P(None, "chan"),
            P("chan", None),
            P("chan", None),
            P(),
        ),
        out_specs=P(None, "chan", "blk"),
        check_vma=False,
    )
```

```python
import math

import jax
import jax.numpy as jnp
from jax import lax
from jax.experimental import pallas as pl
from jax.experimental.pallas import tpu as pltpu
from jax.sharding import PartitionSpec as P

slab_width = 5.0 / 3.0
cross_width = 48.0
cut_radius = 5.0
soften = 0.25
components = 9
orders = ((0, 1), (1, 4), (4, 9))
lanes = 128
tile = 16

cos_terms = (
    -0.6056998671923182,
    -0.8837930130905377,
    0.5945743675766054,
    -0.11556393696983189,
    0.011100594647768918,
    -0.0006430391121701238,
    2.490485442655993e-05,
)
sinc_terms = (
    0.22505602342469963,
    -0.30281424022132397,
    0.08828480791644601,
    -0.011306965460218523,
    0.0008171987621448651,
    -3.805921488925154e-05,
    1.2352514278347018e-06,
)


def horner(terms, v):
    value = jnp.full_like(v, terms[-1])
    for term in terms[-2::-1]:
        value = value * v + term
    return value


def pair_rows(own, other, box_x, count, apart):
    shift = []
    for axis, length in enumerate((box_x, cross_width, cross_width)):
        r = other[axis] - own[axis]
        shift.append(r - length * jnp.floor(r * (1.0 / length) + 0.5))
    x, y, z = shift
    xx, yy, zz = x * x, y * y, z * z
    s = xx + yy + zz + soften
    inverse = lax.rsqrt(s)
    d = s * inverse
    scaled = d * (1.0 / cut_radius)
    square = s * (1.0 / cut_radius**2)
    sixth = square * square * square
    envelope = 1.0 + sixth * (scaled * 48.0 - 28.0 - 21.0 * square)
    keep = s < cut_radius**2
    if apart is not None:
        keep = jnp.logical_and(keep, apart)
    v = s * (2.0 / cut_radius**2) - 1.0
    first = jnp.where(keep, envelope * math.sqrt(2.0 / cut_radius), 0.0) * horner(sinc_terms, v)
    twice = 2.0 * horner(cos_terms, v)
    radial = [first, twice * first]
    while len(radial) < count:
        radial.append(twice * radial[-1] - radial[-2])
    root3, root15 = math.sqrt(3.0), math.sqrt(15.0)
    over = inverse * inverse
    s15 = root15 * over
    over3 = root3 * inverse
    harmonics = [
        None,
        x * over3,
        y * over3,
        z * over3,
        x * y * s15,
        y * z * s15,
        (2.0 * zz - xx - yy) * (0.5 * math.sqrt(5.0) * over),
        x * z * s15,
        (xx - yy) * (0.5 * s15),
    ]
    return [[r if h is None else r * h for h in harmonics] for r in radial[:count]]


def pair_kernel(slabs, data_count, own_slab, first, last, box_x, count, *refs):
    refs = list(refs)
    pos_ref, act_ref, par_ref = refs[:3]
    data = refs[3 : 3 + data_count]
    rest = refs[3 + data_count :]
    if not first:
        acc_ref = rest.pop(0)
    if last:
        mix_ref = rest.pop(0)
    out_ref, table_ref, weight_ref, sum_ref = rest
    channels = par_ref.shape[0]
    own = [jnp.broadcast_to(pos_ref[axis : axis + 1, :], (tile, lanes)) for axis in range(3)]
    for place, (which, base, index) in enumerate(slabs):
        ref = data[which]
        feats = ref[base : base + channels, :] * act_ref[index : index + 1, :]
        columns = ref[base + channels : base + channels + 8, :].T
        for n in range(count):
            weight_ref[:, n * lanes : (n + 1) * lanes] = (par_ref[:, n : n + 1] * feats).astype(
                jnp.bfloat16
            )
        for step in range(lanes // tile):
            rows = slice(step * tile, (step + 1) * tile)
            other = [
                jnp.broadcast_to(columns[rows, axis : axis + 1], (tile, lanes)) for axis in range(3)
            ]
            apart = None
            if index == own_slab:
                apart = (
                    lax.broadcasted_iota(jnp.int32, (tile, lanes), 0) + step * tile
                ) != lax.broadcasted_iota(jnp.int32, (tile, lanes), 1)
            table = pair_rows(own, other, box_x, count, apart)
            for n in range(count):
                for m in range(components):
                    table_ref[
                        n * lanes + step * tile : n * lanes + (step + 1) * tile,
                        m * lanes : (m + 1) * lanes,
                    ] = table[n][m].astype(jnp.bfloat16)
        part = jnp.dot(weight_ref[...], table_ref[...], preferred_element_type=jnp.float32)
        target = out_ref if not last else sum_ref
        if place == 0:
            target[...] = part if first else acc_ref[...] + part
        else:
            target[...] += part
    if not last:
        return
    kinds = par_ref.shape[1] - count
    centre = jnp.zeros((channels, lanes), jnp.float32)
    for kind in range(kinds):
        here = pos_ref[3:4, :] == float(kind)
        centre = jnp.where(here, par_ref[:, count + kind : count + kind + 1], centre)
    for order, (start, stop) in enumerate(orders):
        mix = mix_ref[order]
        mix_high = mix.astype(jnp.bfloat16)
        mix_low = (mix - mix_high.astype(jnp.float32)).astype(jnp.bfloat16)
        total = None
        for m in range(start, stop):
            features = sum_ref[:, m * lanes : (m + 1) * lanes] * centre
            high = features.astype(jnp.bfloat16)
            low = (features - high.astype(jnp.float32)).astype(jnp.bfloat16)
            mixed = (
                jnp.dot(mix_high, high, preferred_element_type=jnp.float32)
                + jnp.dot(mix_high, low, preferred_element_type=jnp.float32)
                + jnp.dot(mix_low, high, preferred_element_type=jnp.float32)
            )
            total = mixed * mixed if total is None else total + mixed * mixed
        out_ref[order] = jnp.log1p(total)


def accumulate(name, pos, act, par, data, slabs, own_slab, box_x, count, acc=None, mix=None):
    channels, atoms = par.shape[0], pos.shape[1]
    operands = [pos, act, par, *data]
    if acc is not None:
        operands.append(acc)
    if mix is not None:
        operands.append(mix)
    wide = (channels, components * atoms)
    shape = wide if mix is None else (mix.shape[0], mix.shape[1], atoms)
    flops = 2 * channels * count * components * atoms * atoms * len(slabs)

    def body(*refs):
        pair_kernel(
            slabs, len(data), own_slab, acc is None, mix is not None, box_x, count, *refs
        )

    return pl.pallas_call(
        body,
        out_shape=jax.ShapeDtypeStruct(shape, jnp.float32),
        in_specs=[pl.BlockSpec(memory_space=pltpu.VMEM)] * len(operands),
        out_specs=pl.BlockSpec(memory_space=pltpu.VMEM),
        scratch_shapes=[
            pltpu.VMEM((count * atoms, components * atoms), jnp.bfloat16),
            pltpu.VMEM((channels, count * atoms), jnp.bfloat16),
            pltpu.VMEM(wide if mix is not None else (8, lanes), jnp.float32),
        ],
        cost_estimate=pl.CostEstimate(flops=flops, bytes_accessed=1 << 20, transcendentals=0),
        compiler_params=pltpu.CompilerParams(vmem_limit_bytes=16 << 20),
        name=name,
    )(*operands)


def pack_kernel(*refs):
    sources, (out_ref, own_ref), held_refs = refs[:6], refs[6:8], refs[8:14]
    tile_ref, sems = refs[14:]
    copies = [
        pltpu.make_async_copy(source, held_ref, sems.at[i])
        for i, (source, held_ref) in enumerate(zip(sources, held_refs))
    ]
    for copy in copies:
        copy.start()
    feats_ref, species_ref, pos_ref, embed_ref, radial_ref, center_ref = held_refs
    held = feats_ref.shape[0]
    kinds, count = embed_ref.shape[0], radial_ref.shape[0]
    tile_ref[...] = jnp.zeros_like(tile_ref)
    out_ref[held:, :] = jnp.zeros((tile, lanes), jnp.float32)
    own_ref[...] = jnp.zeros_like(own_ref)
    for copy in copies:
        copy.wait()
    tile_ref[0:kinds, 0:held] = embed_ref[...]
    columns = tile_ref[...].T
    embedded = jnp.zeros(feats_ref.shape, jnp.float32)
    for kind in range(kinds):
        embedded = jnp.where(species_ref[...] == kind, columns[:held, kind : kind + 1], embedded)
    out_ref[0:held, :] = feats_ref[...] * embedded
    out_ref[held : held + count, 0:held] = radial_ref[...]
    out_ref[held + count : held + count + kinds, 0:held] = center_ref[...]
    own_ref[0:3, :] = pos_ref[...]
    own_ref[3:4, :] = species_ref[...].astype(jnp.float32)


def pack(node_features, species, positions, species_embed, radial_weight, center_embed):
    held, atoms = node_features.shape
    operands = (
        node_features,
        species[None],
        positions,
        species_embed.T,
        radial_weight,
        center_embed.T,
    )
    return pl.pallas_call(
        pack_kernel,
        out_shape=(
            jax.ShapeDtypeStruct((held + tile, atoms), jnp.float32),
            jax.ShapeDtypeStruct((8, atoms), jnp.float32),
        ),
        in_specs=[pl.BlockSpec(memory_space=pltpu.HBM)] * len(operands),
        out_specs=[pl.BlockSpec(memory_space=pltpu.VMEM)] * 2,
        scratch_shapes=[pltpu.VMEM(x.shape, x.dtype) for x in operands]
        + [pltpu.VMEM((8, lanes), jnp.float32), pltpu.SemaphoreType.DMA((len(operands),))],
        compiler_params=pltpu.CompilerParams(vmem_limit_bytes=1 << 20),
        name="pack",
    )(*operands)


def moved(value, axis, target):
    size = lax.axis_size(axis)
    return lax.ppermute(value, axis, [(i, target(i, size)) for i in range(size)])


def flipped(value, axis, bit):
    return moved(value, axis, lambda i, size: i ^ bit)


def shards(
    positions,
    species,
    node_features,
    block_mask,
    radial_weight,
    species_embed,
    center_embed,
    mix_weight,
):
    slab_count = lax.axis_size("blk")
    owner_count = lax.axis_size("chan")
    box_x = float(slab_count) * slab_width
    reach = (block_mask.shape[1] - 1) // 2
    count = radial_weight.shape[0]
    kinds = species_embed.shape[1]
    held, atoms = node_features.shape
    me = lax.axis_index("blk")
    owner = lax.axis_index("chan")

    owned, pos = pack(
        node_features, species, positions, species_embed, radial_weight, center_embed
    )
    owned = owned[None]
    bit = owner_count // 2
    flips = [0]
    while bit:
        owned = jnp.concatenate([owned, flipped(owned, "chan", bit)], axis=0)
        flips = flips + [f ^ bit for f in flips]
        bit //= 2
    channels = held * owner_count
    feats = owned[:, :held].reshape(channels, atoms)
    par = owned[:, held : held + count + kinds, :held].transpose(0, 2, 1)
    par = par.reshape(channels, count + kinds)
    mine = lax.dynamic_slice_in_dim(mix_weight, owner * held, held, 1)
    mix = jnp.concatenate(
        [lax.dynamic_slice_in_dim(mine, (owner ^ f) * held, held, 2) for f in flips], axis=2
    )

    bundle = jnp.concatenate([feats, pos], axis=0)
    depth = bundle.shape[0]

    def activity(places):
        offset = jnp.stack([lax.rem(p - me + reach + slab_count, slab_count) for p in places])
        at = offset[:, None] == jnp.arange(2 * reach + 1, dtype=jnp.int32)[None, :]
        value = jnp.sum(jnp.where(at, block_mask, 0), axis=1).astype(jnp.float32)
        return jnp.broadcast_to(value[:, None], (len(places), atoms))

    call = lambda name, act, data, slabs, acc=None, mix=None: accumulate(
        name, pos, act, par, data, slabs, 0, box_x, count, acc, mix
    )
    if slab_count == 2 * (reach + 1) == 8:
        act = activity([me ^ j for j in range(slab_count)])
        two = flipped(bundle, "blk", 2)
        acc = call("own", act, [bundle], [(0, 0, 0)])
        two, acc = lax.optimization_barrier((two, acc))
        pair = jnp.concatenate([bundle, two], axis=0)
        four = flipped(pair, "blk", 4)
        one = flipped(pair, "blk", 1)
        acc = call("two", act, [two], [(0, 0, 2)], acc)
        acc = call("one", act, [one], [(0, 0, 1)], acc)
        four, acc = lax.optimization_barrier((four, acc))
        five = flipped(four, "blk", 1)
        acc = call("three", act, [one], [(0, depth, 3)], acc)
        five, acc = lax.optimization_barrier((five, acc))
        return call(
            "far", act, [four, five], [(0, depth, 6), (1, 0, 5), (1, depth, 7)], acc, mix
        )
    places = [0] + [k for h in range(1, reach + 1) for k in (h, -h)]
    act = activity([lax.rem(me + k + slab_count, slab_count) for k in places])
    act = jnp.pad(act, ((0, 8 - len(places)), (0, 0)))
    data = [bundle] + [
        moved(bundle, "blk", lambda i, size, k=k: (i - k) % size) for k in places[1:]
    ]
    return call("all", act, data, [(j, 0, j) for j in range(len(places))], None, mix)


def solution(mesh):
    return jax.shard_map(
        shards,
        mesh=mesh,
        in_specs=(
            P(None, "blk"),
            P("blk"),
            P("chan", "blk"),
            P("blk", None),
            P(None, "chan"),
            P("chan", None),
            P("chan", None),
            P(),
        ),
        out_specs=P(None, "chan", "blk"),
        check_vma=False,
    )
```

```python
import math

import jax
import jax.numpy as jnp
from jax import lax
from jax.experimental import pallas as pl
from jax.experimental.pallas import tpu as pltpu
from jax.sharding import PartitionSpec as P

slab_width = 5.0 / 3.0
cross_width = 48.0
cut_radius = 5.0
soften = 0.25
components = 9
orders = ((0, 1), (1, 4), (4, 9))
lanes = 128
tile = 16

cos_terms = (
    -0.6056998671923182,
    -0.8837930130905377,
    0.5945743675766054,
    -0.11556393696983189,
    0.011100594647768918,
    -0.0006430391121701238,
    2.490485442655993e-05,
)
sinc_terms = (
    0.22505602342469963,
    -0.30281424022132397,
    0.08828480791644601,
    -0.011306965460218523,
    0.0008171987621448651,
    -3.805921488925154e-05,
    1.2352514278347018e-06,
)


def horner(terms, v):
    value = jnp.full_like(v, terms[-1])
    for term in terms[-2::-1]:
        value = value * v + term
    return value


def pair_rows(own, other, box_x, count, apart):
    shift = []
    for axis, length in enumerate((box_x, cross_width, cross_width)):
        r = other[axis] - own[axis]
        shift.append(r - length * jnp.floor(r * (1.0 / length) + 0.5))
    x, y, z = shift
    xx, yy, zz = x * x, y * y, z * z
    s = xx + yy + zz + soften
    inverse = lax.rsqrt(s)
    d = s * inverse
    scaled = d * (1.0 / cut_radius)
    square = s * (1.0 / cut_radius**2)
    sixth = square * square * square
    envelope = 1.0 + sixth * (scaled * 48.0 - 28.0 - 21.0 * square)
    keep = s < cut_radius**2
    if apart is not None:
        keep = jnp.logical_and(keep, apart)
    v = s * (2.0 / cut_radius**2) - 1.0
    first = jnp.where(keep, envelope * math.sqrt(2.0 / cut_radius), 0.0) * horner(sinc_terms, v)
    twice = 2.0 * horner(cos_terms, v)
    radial = [first, twice * first]
    while len(radial) < count:
        radial.append(twice * radial[-1] - radial[-2])
    root3, root15 = math.sqrt(3.0), math.sqrt(15.0)
    over = inverse * inverse
    s15 = root15 * over
    over3 = root3 * inverse
    harmonics = [
        None,
        x * over3,
        y * over3,
        z * over3,
        x * y * s15,
        y * z * s15,
        (2.0 * zz - xx - yy) * (0.5 * math.sqrt(5.0) * over),
        x * z * s15,
        (xx - yy) * (0.5 * s15),
    ]
    return [[r if h is None else r * h for h in harmonics] for r in radial[:count]]


def pair_kernel(slabs, data_count, own_slab, first, last, box_x, count, *refs):
    refs = list(refs)
    pos_ref, act_ref, par_ref = refs[:3]
    data = refs[3 : 3 + data_count]
    rest = refs[3 + data_count :]
    if not first:
        acc_ref = rest.pop(0)
    if last:
        mix_ref = rest.pop(0)
    out_ref, table_ref, weight_ref, sum_ref = rest
    channels = par_ref.shape[0]
    own = [jnp.broadcast_to(pos_ref[axis : axis + 1, :], (tile, lanes)) for axis in range(3)]
    for place, (which, base, index) in enumerate(slabs):
        ref = data[which]
        feats = ref[base : base + channels, :] * act_ref[index : index + 1, :]
        columns = ref[base + channels : base + channels + 8, :].T
        for n in range(count):
            weight_ref[:, n * lanes : (n + 1) * lanes] = (par_ref[:, n : n + 1] * feats).astype(
                jnp.bfloat16
            )
        for step in range(lanes // tile):
            rows = slice(step * tile, (step + 1) * tile)
            other = [
                jnp.broadcast_to(columns[rows, axis : axis + 1], (tile, lanes)) for axis in range(3)
            ]
            apart = None
            if index == own_slab:
                apart = (
                    lax.broadcasted_iota(jnp.int32, (tile, lanes), 0) + step * tile
                ) != lax.broadcasted_iota(jnp.int32, (tile, lanes), 1)
            table = pair_rows(own, other, box_x, count, apart)
            for n in range(count):
                for m in range(components):
                    table_ref[
                        n * lanes + step * tile : n * lanes + (step + 1) * tile,
                        m * lanes : (m + 1) * lanes,
                    ] = table[n][m].astype(jnp.bfloat16)
        part = jnp.dot(weight_ref[...], table_ref[...], preferred_element_type=jnp.float32)
        target = out_ref if not last else sum_ref
        if place == 0:
            target[...] = part if first else acc_ref[...] + part
        else:
            target[...] += part
    if not last:
        return
    kinds = par_ref.shape[1] - count
    centre = jnp.zeros((channels, lanes), jnp.float32)
    for kind in range(kinds):
        here = pos_ref[3:4, :] == float(kind)
        centre = jnp.where(here, par_ref[:, count + kind : count + kind + 1], centre)
    for order, (start, stop) in enumerate(orders):
        mix = mix_ref[order]
        mix_high = mix.astype(jnp.bfloat16)
        mix_low = (mix - mix_high.astype(jnp.float32)).astype(jnp.bfloat16)
        total = None
        for m in range(start, stop):
            features = sum_ref[:, m * lanes : (m + 1) * lanes] * centre
            high = features.astype(jnp.bfloat16)
            low = (features - high.astype(jnp.float32)).astype(jnp.bfloat16)
            mixed = (
                jnp.dot(mix_high, high, preferred_element_type=jnp.float32)
                + jnp.dot(mix_high, low, preferred_element_type=jnp.float32)
                + jnp.dot(mix_low, high, preferred_element_type=jnp.float32)
            )
            total = mixed * mixed if total is None else total + mixed * mixed
        out_ref[order] = jnp.log1p(total)


def accumulate(name, pos, act, par, data, slabs, own_slab, box_x, count, acc=None, mix=None):
    channels, atoms = par.shape[0], pos.shape[1]
    operands = [pos, act, par, *data]
    if acc is not None:
        operands.append(acc)
    if mix is not None:
        operands.append(mix)
    wide = (channels, components * atoms)
    shape = wide if mix is None else (mix.shape[0], mix.shape[1], atoms)
    flops = 2 * channels * count * components * atoms * atoms * len(slabs)

    def body(*refs):
        pair_kernel(
            slabs, len(data), own_slab, acc is None, mix is not None, box_x, count, *refs
        )

    return pl.pallas_call(
        body,
        out_shape=jax.ShapeDtypeStruct(shape, jnp.float32),
        in_specs=[pl.BlockSpec(memory_space=pltpu.VMEM)] * len(operands),
        out_specs=pl.BlockSpec(memory_space=pltpu.VMEM),
        scratch_shapes=[
            pltpu.VMEM((count * atoms, components * atoms), jnp.bfloat16),
            pltpu.VMEM((channels, count * atoms), jnp.bfloat16),
            pltpu.VMEM(wide if mix is not None else (8, lanes), jnp.float32),
        ],
        cost_estimate=pl.CostEstimate(flops=flops, bytes_accessed=1 << 20, transcendentals=0),
        compiler_params=pltpu.CompilerParams(vmem_limit_bytes=16 << 20),
        name=name,
    )(*operands)


def pack_kernel(*refs):
    sources, (out_ref, own_ref), held_refs = refs[:6], refs[6:8], refs[8:14]
    tile_ref, sems = refs[14:]
    copies = [
        pltpu.make_async_copy(source, held_ref, sems.at[i])
        for i, (source, held_ref) in enumerate(zip(sources, held_refs))
    ]
    for copy in copies:
        copy.start()
    feats_ref, species_ref, pos_ref, embed_ref, radial_ref, center_ref = held_refs
    held = feats_ref.shape[0]
    kinds, count = embed_ref.shape[0], radial_ref.shape[0]
    tile_ref[...] = jnp.zeros_like(tile_ref)
    out_ref[held:, :] = jnp.zeros((tile, lanes), jnp.float32)
    own_ref[...] = jnp.zeros_like(own_ref)
    for copy in copies:
        copy.wait()
    tile_ref[0:kinds, 0:held] = embed_ref[...]
    columns = tile_ref[...].T
    embedded = jnp.zeros(feats_ref.shape, jnp.float32)
    for kind in range(kinds):
        embedded = jnp.where(species_ref[...] == kind, columns[:held, kind : kind + 1], embedded)
    out_ref[0:held, :] = feats_ref[...] * embedded
    out_ref[held : held + count, 0:held] = radial_ref[...]
    out_ref[held + count : held + count + kinds, 0:held] = center_ref[...]
    own_ref[0:3, :] = pos_ref[...]
    own_ref[3:4, :] = species_ref[...].astype(jnp.float32)


def pack(node_features, species, positions, species_embed, radial_weight, center_embed):
    held, atoms = node_features.shape
    operands = (
        node_features,
        species[None],
        positions,
        species_embed.T,
        radial_weight,
        center_embed.T,
    )
    operands = [pltpu.with_memory_space_constraint(x, pltpu.HBM) for x in operands]
    return pl.pallas_call(
        pack_kernel,
        out_shape=(
            jax.ShapeDtypeStruct((held + tile, atoms), jnp.float32),
            jax.ShapeDtypeStruct((8, atoms), jnp.float32),
        ),
        in_specs=[pl.BlockSpec(memory_space=pltpu.HBM)] * len(operands),
        out_specs=[pl.BlockSpec(memory_space=pltpu.VMEM)] * 2,
        scratch_shapes=[pltpu.VMEM(x.shape, x.dtype) for x in operands]
        + [pltpu.VMEM((8, lanes), jnp.float32), pltpu.SemaphoreType.DMA((len(operands),))],
        compiler_params=pltpu.CompilerParams(vmem_limit_bytes=1 << 20),
        name="pack",
    )(*operands)


def moved(value, axis, target):
    size = lax.axis_size(axis)
    return lax.ppermute(value, axis, [(i, target(i, size)) for i in range(size)])


def flipped(value, axis, bit):
    return moved(value, axis, lambda i, size: i ^ bit)


def shards(
    positions,
    species,
    node_features,
    block_mask,
    radial_weight,
    species_embed,
    center_embed,
    mix_weight,
):
    slab_count = lax.axis_size("blk")
    owner_count = lax.axis_size("chan")
    box_x = float(slab_count) * slab_width
    reach = (block_mask.shape[1] - 1) // 2
    count = radial_weight.shape[0]
    kinds = species_embed.shape[1]
    held, atoms = node_features.shape
    me = lax.axis_index("blk")
    owner = lax.axis_index("chan")

    owned, pos = pack(
        node_features, species, positions, species_embed, radial_weight, center_embed
    )
    owned = owned[None]
    bit = owner_count // 2
    flips = [0]
    while bit:
        owned = jnp.concatenate([owned, flipped(owned, "chan", bit)], axis=0)
        flips = flips + [f ^ bit for f in flips]
        bit //= 2
    channels = held * owner_count
    feats = owned[:, :held].reshape(channels, atoms)
    par = owned[:, held : held + count + kinds, :held].transpose(0, 2, 1)
    par = par.reshape(channels, count + kinds)
    mine = lax.dynamic_slice_in_dim(mix_weight, owner * held, held, 1)
    mix = jnp.concatenate(
        [lax.dynamic_slice_in_dim(mine, (owner ^ f) * held, held, 2) for f in flips], axis=2
    )

    bundle = jnp.concatenate([feats, pos], axis=0)
    depth = bundle.shape[0]

    def activity(places):
        offset = jnp.stack([lax.rem(p - me + reach + slab_count, slab_count) for p in places])
        at = offset[:, None] == jnp.arange(2 * reach + 1, dtype=jnp.int32)[None, :]
        value = jnp.sum(jnp.where(at, block_mask, 0), axis=1).astype(jnp.float32)
        return jnp.broadcast_to(value[:, None], (len(places), atoms))

    call = lambda name, act, data, slabs, acc=None, mix=None: accumulate(
        name, pos, act, par, data, slabs, 0, box_x, count, acc, mix
    )
    if slab_count == 2 * (reach + 1) == 8:
        act = activity([me ^ j for j in range(slab_count)])
        three = flipped(bundle, "blk", 3)
        acc = call("own", act, [bundle], [(0, 0, 0)])
        three, acc = lax.optimization_barrier((three, acc))
        pair = jnp.concatenate([bundle, three], axis=0)
        five = flipped(pair, "blk", 5)
        one = flipped(pair, "blk", 1)
        acc = call("near", act, [three], [(0, 0, 3)], acc)
        acc = call("middle", act, [one], [(0, 0, 1), (0, depth, 2)], acc)
        five, acc = lax.optimization_barrier((five, acc))
        seven = flipped(five[depth:], "blk", 1)
        acc = call("next", act, [five], [(0, 0, 5)], acc)
        seven, acc = lax.optimization_barrier((seven, acc))
        return call("far", act, [five, seven], [(0, depth, 6), (1, 0, 7)], acc, mix)
    places = [0] + [k for h in range(1, reach + 1) for k in (h, -h)]
    act = activity([lax.rem(me + k + slab_count, slab_count) for k in places])
    act = jnp.pad(act, ((0, 8 - len(places)), (0, 0)))
    data = [bundle] + [
        moved(bundle, "blk", lambda i, size, k=k: (i - k) % size) for k in places[1:]
    ]
    return call("all", act, data, [(j, 0, j) for j in range(len(places))], None, mix)


def solution(mesh):
    return jax.shard_map(
        shards,
        mesh=mesh,
        in_specs=(
            P(None, "blk"),
            P("blk"),
            P("chan", "blk"),
            P("blk", None),
            P(None, "chan"),
            P("chan", None),
            P("chan", None),
            P(),
        ),
        out_specs=P(None, "chan", "blk"),
        check_vma=False,
    )
```

```python
import math

import jax
import jax.numpy as jnp
from jax import lax
from jax.experimental import pallas as pl
from jax.experimental.pallas import tpu as pltpu
from jax.sharding import PartitionSpec as P

slab_width = 5.0 / 3.0
cross_width = 48.0
cut_radius = 5.0
soften = 0.25
components = 9
orders = ((0, 1), (1, 4), (4, 9))
lanes = 128
tile = 16

cos_terms = (
    -0.6056998671923182,
    -0.8837930130905377,
    0.5945743675766054,
    -0.11556393696983189,
    0.011100594647768918,
    -0.0006430391121701238,
    2.490485442655993e-05,
)
sinc_terms = (
    0.22505602342469963,
    -0.30281424022132397,
    0.08828480791644601,
    -0.011306965460218523,
    0.0008171987621448651,
    -3.805921488925154e-05,
    1.2352514278347018e-06,
)


def horner(terms, v):
    value = jnp.full_like(v, terms[-1])
    for term in terms[-2::-1]:
        value = value * v + term
    return value


def pair_rows(own, other, box_x, count, apart):
    shift = []
    for axis, length in enumerate((box_x, cross_width, cross_width)):
        r = other[axis] - own[axis]
        shift.append(length * (r - jnp.round(r)))
    x, y, z = shift
    xx, yy, zz = x * x, y * y, z * z
    s = xx + yy + zz + soften
    inverse = lax.rsqrt(s)
    d = s * inverse
    scaled = d * (1.0 / cut_radius)
    square = s * (1.0 / cut_radius**2)
    sixth = square * square * square
    envelope = 1.0 + sixth * (scaled * 48.0 - 28.0 - 21.0 * square)
    keep = s < cut_radius**2
    if apart is not None:
        keep = jnp.logical_and(keep, apart)
    v = s * (2.0 / cut_radius**2) - 1.0
    first = jnp.where(keep, envelope * math.sqrt(2.0 / cut_radius), 0.0) * horner(sinc_terms, v)
    twice = 2.0 * horner(cos_terms, v)
    radial = [first, twice * first]
    while len(radial) < count:
        radial.append(twice * radial[-1] - radial[-2])
    root3, root15 = math.sqrt(3.0), math.sqrt(15.0)
    over = inverse * inverse
    s15 = root15 * over
    over3 = root3 * inverse
    harmonics = [
        None,
        x * over3,
        y * over3,
        z * over3,
        x * y * s15,
        y * z * s15,
        (2.0 * zz - xx - yy) * (0.5 * math.sqrt(5.0) * over),
        x * z * s15,
        (xx - yy) * (0.5 * s15),
    ]
    radial = [r.astype(jnp.bfloat16) for r in radial[:count]]
    harmonics = [None if h is None else h.astype(jnp.bfloat16) for h in harmonics]
    return [[r if h is None else r * h for h in harmonics] for r in radial]


def pair_kernel(slabs, data_count, own_slab, first, last, box_x, count, *refs):
    refs = list(refs)
    pos_ref, act_ref, par_ref = refs[:3]
    data = refs[3 : 3 + data_count]
    rest = refs[3 + data_count :]
    if not first:
        acc_ref = rest.pop(0)
    if last:
        mix_ref = rest.pop(0)
    out_ref, sum_ref = rest
    channels = par_ref.shape[0]
    scale = [1.0 / box_x, 1.0 / cross_width, 1.0 / cross_width]
    own = [
        jnp.broadcast_to(pos_ref[axis : axis + 1, :] * scale[axis], (tile, lanes))
        for axis in range(3)
    ]
    lane = lax.broadcasted_iota(jnp.int32, (channels, lanes), 1)
    group, within = lane // tile, lax.rem(lane, tile)
    spread = jnp.broadcast_to(par_ref[:, 0:1], (channels, lanes))
    for n in range(1, count):
        spread = jnp.where(group == n, par_ref[:, n : n + 1], spread)
    for place, (which, base, index) in enumerate(slabs):
        ref = data[which]
        feats = ref[base : base + channels, :] * act_ref[index : index + 1, :]
        columns = ref[base + channels : base + channels + 8, :].T
        part = None
        for pair in range(lanes // (2 * tile)):
            weights, tables = [], []
            for step in (2 * pair, 2 * pair + 1):
                picked = jnp.take_along_axis(feats, within + step * tile, axis=1)
                weights.append((spread * picked).astype(jnp.bfloat16))
                rows = slice(step * tile, (step + 1) * tile)
                other = [
                    jnp.broadcast_to(columns[rows, axis : axis + 1] * scale[axis], (tile, lanes))
                    for axis in range(3)
                ]
                apart = None
                if index == own_slab:
                    apart = (
                        lax.broadcasted_iota(jnp.int32, (tile, lanes), 0) + step * tile
                    ) != lax.broadcasted_iota(jnp.int32, (tile, lanes), 1)
                tables += pair_rows(own, other, box_x, count, apart)
            stacked = jnp.concatenate([jnp.concatenate(row, axis=1) for row in tables], axis=0)
            product = jnp.dot(
                jnp.concatenate(weights, axis=1), stacked, preferred_element_type=jnp.float32
            )
            part = product if part is None else part + product
        target = out_ref if not last else sum_ref
        if place == 0:
            target[...] = part if first else acc_ref[...] + part
        else:
            target[...] += part
    if not last:
        return
    kinds = par_ref.shape[1] - count
    centre = jnp.zeros((channels, lanes), jnp.float32)
    for kind in range(kinds):
        here = pos_ref[3:4, :] == float(kind)
        centre = jnp.where(here, par_ref[:, count + kind : count + kind + 1], centre)
    for order, (start, stop) in enumerate(orders):
        mix = mix_ref[order]
        mix_high = mix.astype(jnp.bfloat16)
        mix_low = (mix - mix_high.astype(jnp.float32)).astype(jnp.bfloat16)
        total = None
        for m in range(start, stop):
            features = sum_ref[:, m * lanes : (m + 1) * lanes] * centre
            high = features.astype(jnp.bfloat16)
            low = (features - high.astype(jnp.float32)).astype(jnp.bfloat16)
            mixed = (
                jnp.dot(mix_high, high, preferred_element_type=jnp.float32)
                + jnp.dot(mix_high, low, preferred_element_type=jnp.float32)
                + jnp.dot(mix_low, high, preferred_element_type=jnp.float32)
            )
            total = mixed * mixed if total is None else total + mixed * mixed
        out_ref[order] = jnp.log1p(total)


def accumulate(name, pos, act, par, data, slabs, own_slab, box_x, count, acc=None, mix=None):
    channels, atoms = par.shape[0], pos.shape[1]
    operands = [pos, act, par, *data]
    if acc is not None:
        operands.append(acc)
    if mix is not None:
        operands.append(mix)
    wide = (channels, components * atoms)
    shape = wide if mix is None else (mix.shape[0], mix.shape[1], atoms)
    flops = 2 * channels * count * components * atoms * atoms * len(slabs)

    def body(*refs):
        pair_kernel(
            slabs, len(data), own_slab, acc is None, mix is not None, box_x, count, *refs
        )

    return pl.pallas_call(
        body,
        out_shape=jax.ShapeDtypeStruct(shape, jnp.float32),
        in_specs=[pl.BlockSpec(memory_space=pltpu.VMEM)] * len(operands),
        out_specs=pl.BlockSpec(memory_space=pltpu.VMEM),
        scratch_shapes=[
            pltpu.VMEM(wide if mix is not None else (8, lanes), jnp.float32),
        ],
        cost_estimate=pl.CostEstimate(flops=flops, bytes_accessed=1 << 20, transcendentals=0),
        compiler_params=pltpu.CompilerParams(vmem_limit_bytes=16 << 20),
        name=name,
    )(*operands)


def pack_kernel(*refs):
    sources, (out_ref, own_ref), held_refs = refs[:6], refs[6:8], refs[8:14]
    tile_ref, sems = refs[14:]
    copies = [
        pltpu.make_async_copy(source, held_ref, sems.at[i])
        for i, (source, held_ref) in enumerate(zip(sources, held_refs))
    ]
    for copy in copies:
        copy.start()
    feats_ref, species_ref, pos_ref, embed_ref, radial_ref, center_ref = held_refs
    held = feats_ref.shape[0]
    kinds, count = embed_ref.shape[0], radial_ref.shape[0]
    tile_ref[...] = jnp.zeros_like(tile_ref)
    out_ref[held:, :] = jnp.zeros((tile, lanes), jnp.float32)
    own_ref[...] = jnp.zeros_like(own_ref)
    for copy in copies:
        copy.wait()
    tile_ref[0:kinds, 0:held] = embed_ref[...]
    columns = tile_ref[...].T
    embedded = jnp.zeros(feats_ref.shape, jnp.float32)
    for kind in range(kinds):
        embedded = jnp.where(species_ref[...] == kind, columns[:held, kind : kind + 1], embedded)
    out_ref[0:held, :] = feats_ref[...] * embedded
    out_ref[held : held + count, 0:held] = radial_ref[...]
    out_ref[held + count : held + count + kinds, 0:held] = center_ref[...]
    own_ref[0:3, :] = pos_ref[...]
    own_ref[3:4, :] = species_ref[...].astype(jnp.float32)


def pack(node_features, species, positions, species_embed, radial_weight, center_embed):
    held, atoms = node_features.shape
    operands = (
        node_features,
        species[None],
        positions,
        species_embed.T,
        radial_weight,
        center_embed.T,
    )
    operands = [pltpu.with_memory_space_constraint(x, pltpu.HBM) for x in operands]
    return pl.pallas_call(
        pack_kernel,
        out_shape=(
            jax.ShapeDtypeStruct((held + tile, atoms), jnp.float32),
            jax.ShapeDtypeStruct((8, atoms), jnp.float32),
        ),
        in_specs=[pl.BlockSpec(memory_space=pltpu.HBM)] * len(operands),
        out_specs=[pl.BlockSpec(memory_space=pltpu.VMEM)] * 2,
        scratch_shapes=[pltpu.VMEM(x.shape, x.dtype) for x in operands]
        + [pltpu.VMEM((8, lanes), jnp.float32), pltpu.SemaphoreType.DMA((len(operands),))],
        compiler_params=pltpu.CompilerParams(vmem_limit_bytes=1 << 20),
        name="pack",
    )(*operands)


def moved(value, axis, target):
    size = lax.axis_size(axis)
    return lax.ppermute(value, axis, [(i, target(i, size)) for i in range(size)])


def flipped(value, axis, bit):
    return moved(value, axis, lambda i, size: i ^ bit)


def shards(
    positions,
    species,
    node_features,
    block_mask,
    radial_weight,
    species_embed,
    center_embed,
    mix_weight,
):
    slab_count = lax.axis_size("blk")
    owner_count = lax.axis_size("chan")
    box_x = float(slab_count) * slab_width
    reach = (block_mask.shape[1] - 1) // 2
    count = radial_weight.shape[0]
    kinds = species_embed.shape[1]
    held, atoms = node_features.shape
    me = lax.axis_index("blk")
    owner = lax.axis_index("chan")

    owned, pos = pack(
        node_features, species, positions, species_embed, radial_weight, center_embed
    )
    owned = owned[None]
    bit = owner_count // 2
    flips = [0]
    while bit:
        owned = jnp.concatenate([owned, flipped(owned, "chan", bit)], axis=0)
        flips = flips + [f ^ bit for f in flips]
        bit //= 2
    channels = held * owner_count
    feats = owned[:, :held].reshape(channels, atoms)
    par = owned[:, held : held + count + kinds, :held].transpose(0, 2, 1)
    par = par.reshape(channels, count + kinds)
    mine = lax.dynamic_slice_in_dim(mix_weight, owner * held, held, 1)
    mix = jnp.concatenate(
        [lax.dynamic_slice_in_dim(mine, (owner ^ f) * held, held, 2) for f in flips], axis=2
    )

    bundle = jnp.concatenate([feats, pos], axis=0)
    depth = bundle.shape[0]

    def activity(places):
        offset = jnp.stack([lax.rem(p - me + reach + slab_count, slab_count) for p in places])
        at = offset[:, None] == jnp.arange(2 * reach + 1, dtype=jnp.int32)[None, :]
        value = jnp.sum(jnp.where(at, block_mask, 0), axis=1).astype(jnp.float32)
        return jnp.broadcast_to(value[:, None], (len(places), atoms))

    call = lambda name, act, data, slabs, acc=None, mix=None: accumulate(
        name, pos, act, par, data, slabs, 0, box_x, count, acc, mix
    )
    if slab_count == 2 * (reach + 1) == 8:
        act = activity([me ^ j for j in range(slab_count)])
        three = flipped(bundle, "blk", 3)
        acc = call("own", act, [bundle], [(0, 0, 0)])
        three, acc = lax.optimization_barrier((three, acc))
        pair = jnp.concatenate([bundle, three], axis=0)
        five = flipped(pair, "blk", 5)
        one = flipped(pair, "blk", 1)
        acc = call("near", act, [three], [(0, 0, 3)], acc)
        acc = call("middle", act, [one], [(0, 0, 1), (0, depth, 2)], acc)
        five, acc = lax.optimization_barrier((five, acc))
        seven = flipped(five[depth:], "blk", 1)
        acc = call("next", act, [five], [(0, 0, 5)], acc)
        seven, acc = lax.optimization_barrier((seven, acc))
        return call("far", act, [five, seven], [(0, depth, 6), (1, 0, 7)], acc, mix)
    places = [0] + [k for h in range(1, reach + 1) for k in (h, -h)]
    act = activity([lax.rem(me + k + slab_count, slab_count) for k in places])
    act = jnp.pad(act, ((0, 8 - len(places)), (0, 0)))
    data = [bundle] + [
        moved(bundle, "blk", lambda i, size, k=k: (i - k) % size) for k in places[1:]
    ]
    return call("all", act, data, [(j, 0, j) for j in range(len(places))], None, mix)


def solution(mesh):
    return jax.shard_map(
        shards,
        mesh=mesh,
        in_specs=(
            P(None, "blk"),
            P("blk"),
            P("chan", "blk"),
            P("blk", None),
            P(None, "chan"),
            P("chan", None),
            P("chan", None),
            P(),
        ),
        out_specs=P(None, "chan", "blk"),
        check_vma=False,
    )
```

```python
import functools
import math

import jax
import jax.numpy as jnp
from jax import lax
from jax.experimental import pallas as pl
from jax.experimental.pallas import tpu as pltpu
from jax.sharding import PartitionSpec as P


slab_width = 5.0 / 3.0
cross_width = 48.0
cut_radius = 5.0
soften = 0.25
components = 9
orders = ((0, 1), (1, 4), (4, 9))
lanes = 128
tile = 16

twice_cos_terms = (
    1.9999999781180455,
    -9.869602249726915,
    8.117389682486351,
    -2.670316860337427,
    0.4700596167989333,
    -0.05071796727719481,
    0.003187821366091919,
)
factors = (1.0, math.sqrt(3.0), math.sqrt(15.0))


def horner(terms, v):
    value = jnp.full_like(v, terms[-1])
    for term in terms[-2::-1]:
        value = value * v + term
    return value


def pair_rows(own, other, lengths, count, apart):
    shift = []
    for axis, length in enumerate(lengths):
        r = other[axis] - own[axis]
        shift.append(length * (r - jnp.round(r)))
    x, y, z = shift
    s = x * x + y * y + z * z + soften
    inverse = lax.rsqrt(s)
    square = s * (1.0 / cut_radius**2)
    sixth = square * square * square
    level = 0.5 * math.sqrt(2.0 / cut_radius)
    envelope = level + sixth * (
        square * (inverse * (48.0 * cut_radius * level) - 21.0 * level) - 28.0 * level
    )
    keep = square < 1.0
    if apart is not None:
        keep = jnp.logical_and(keep, apart)
    twice = horner(twice_cos_terms, square)
    rest = jnp.maximum(4.0 - twice * twice, 1e-12)
    sine = rest * lax.rsqrt(rest)
    first = jnp.where(keep, envelope, 0.0) * (sine * inverse)
    radial = [first, twice * first]
    while len(radial) < count:
        radial.append(twice * radial[-1] - radial[-2])
    x, y, z = x * inverse, y * inverse, z * inverse
    xx, yy = x * x, y * y
    harmonics = [
        None,
        x,
        y,
        z,
        x * y,
        y * z,
        z * z * (1.0 / math.sqrt(3.0)) - (xx + yy) * (0.5 / math.sqrt(3.0)),
        x * z,
        (xx - yy) * 0.5,
    ]
    radial = [r.astype(jnp.bfloat16) for r in radial[:count]]
    harmonics = [None if h is None else h.astype(jnp.bfloat16) for h in harmonics]
    return [[r if h is None else r * h for h in harmonics] for r in radial]


def pair_kernel(slabs, data_count, own_slab, first, last, box_x, count, *refs):
    refs = list(refs)
    pos_ref, act_ref = refs[:2]
    data = refs[2 : 2 + data_count]
    rest = refs[2 + data_count :]
    lengths = (box_x, cross_width, cross_width)
    own = [jnp.broadcast_to(pos_ref[axis : axis + 1, :], (tile, lanes)) for axis in range(3)]
    channels = rest[0].shape[0]
    lane = lax.broadcasted_iota(jnp.int32, (channels, lanes), 1)
    group, within = lane // tile, lax.rem(lane, tile)
    if first:
        par_ref = rest.pop(0)
        spread = jnp.broadcast_to(par_ref[:, 0:1], (channels, lanes))
        for n in range(1, count):
            spread = jnp.where(group == n, par_ref[:, n : n + 1], spread)
        centre = jnp.zeros((channels, lanes), jnp.float32)
        for kind in range(par_ref.shape[1] - count):
            here = pos_ref[3:4, :] == float(kind)
            centre = jnp.where(here, par_ref[:, count + kind : count + kind + 1], centre)
    else:
        acc_ref, spread_ref, centre_ref = rest.pop(0), rest.pop(0), rest.pop(0)
        spread = spread_ref[...]
    if last:
        mix_ref, out_ref, sum_ref = rest
    elif first:
        sum_ref, spread_ref, centre_ref = rest
        spread_ref[...] = spread
        centre_ref[...] = centre
    else:
        (sum_ref,) = rest
    part = None
    for which, base, index in slabs:
        ref = data[which]
        feats = ref[base : base + channels, :] * act_ref[index : index + 1, :]
        columns = ref[base + channels : base + channels + 8, :].T
        for pair in range(lanes // (2 * tile)):
            weights, tables = [], []
            for step in (2 * pair, 2 * pair + 1):
                picked = jnp.take_along_axis(feats, within + step * tile, axis=1)
                weights.append((spread * picked).astype(jnp.bfloat16))
                rows = slice(step * tile, (step + 1) * tile)
                other = [
                    jnp.broadcast_to(columns[rows, axis : axis + 1], (tile, lanes))
                    for axis in range(3)
                ]
                apart = None
                if index == own_slab:
                    apart = (
                        lax.broadcasted_iota(jnp.int32, (tile, lanes), 0) + step * tile
                    ) != lax.broadcasted_iota(jnp.int32, (tile, lanes), 1)
                tables += pair_rows(own, other, lengths, count, apart)
            stacked = jnp.concatenate([jnp.concatenate(row, axis=1) for row in tables], axis=0)
            product = jnp.dot(
                jnp.concatenate(weights, axis=1), stacked, preferred_element_type=jnp.float32
            )
            part = product if part is None else part + product
    sum_ref[...] = part if first else acc_ref[...] + part
    if not last:
        return
    if not first:
        centre = centre_ref[...]
    held = mix_ref.shape[1]
    for order, (start, stop) in enumerate(orders):
        mix = mix_ref[order] * factors[order]
        mix_high = mix.astype(jnp.bfloat16)
        mix_low = (mix - mix_high.astype(jnp.float32)).astype(jnp.bfloat16)
        features = [sum_ref[:, m * lanes : (m + 1) * lanes] * centre for m in range(start, stop)]
        features = features[0] if len(features) == 1 else jnp.concatenate(features, axis=1)
        high = features.astype(jnp.bfloat16)
        low = (features - high.astype(jnp.float32)).astype(jnp.bfloat16)
        both = jnp.dot(
            jnp.concatenate([mix_high, mix_low], axis=0), high, preferred_element_type=jnp.float32
        )
        mixed = both[:held] + both[held:]
        mixed = mixed + jnp.dot(mix_high, low, preferred_element_type=jnp.float32)
        total = None
        for m in range(stop - start):
            one = mixed[:, m * lanes : (m + 1) * lanes]
            total = one * one if total is None else total + one * one
        out_ref[order] = jnp.log1p(total)


def accumulate(pos, act, data, slabs, own_slab, box_x, count, start, mix=None):
    atoms = pos.shape[1]
    first, last = not isinstance(start, tuple), mix is not None
    channels = (start if first else start[1]).shape[0]
    operands = [pos, act, *data, *((start,) if first else start)]
    wide = jax.ShapeDtypeStruct((channels, components * atoms), jnp.float32)
    narrow = jax.ShapeDtypeStruct((channels, atoms), jnp.float32)
    if last:
        operands.append(mix)
        shapes = jax.ShapeDtypeStruct((len(orders), mix.shape[1], atoms), jnp.float32)
    else:
        shapes = [wide, narrow, narrow] if first else [wide]
    flops = 2 * channels * count * components * atoms * atoms * len(slabs)

    def body(*refs):
        pair_kernel(slabs, len(data), own_slab, first, last, box_x, count, *refs)

    whole = pl.BlockSpec(memory_space=pltpu.VMEM)
    result = pl.pallas_call(
        body,
        out_shape=shapes,
        in_specs=[whole] * len(operands),
        out_specs=whole if last else [whole] * len(shapes),
        scratch_shapes=[pltpu.VMEM(wide.shape, jnp.float32)] if last else [],
        cost_estimate=pl.CostEstimate(flops=flops, bytes_accessed=1 << 20, transcendentals=0),
        compiler_params=pltpu.CompilerParams(vmem_limit_bytes=16 << 20),
    )(*operands)
    return result if last else tuple(result) if first else (result[0], *start[1:])


def pack_kernel(box_x, *refs):
    sources, (out_ref, own_ref), held_refs = refs[:6], refs[6:8], refs[8:14]
    tile_ref, sems = refs[14:]
    copies = [
        pltpu.make_async_copy(source, held_ref, sems.at[i])
        for i, (source, held_ref) in enumerate(zip(sources, held_refs))
    ]
    for copy in copies:
        copy.start()
    feats_ref, species_ref, pos_ref, embed_ref, radial_ref, center_ref = held_refs
    held = feats_ref.shape[0]
    kinds, count = embed_ref.shape[0], radial_ref.shape[0]
    tile_ref[...] = jnp.zeros_like(tile_ref)
    out_ref[held:, :] = jnp.zeros((tile, lanes), jnp.float32)
    own_ref[...] = jnp.zeros_like(own_ref)
    for copy in copies:
        copy.wait()
    tile_ref[0:kinds, 0:held] = embed_ref[...]
    columns = tile_ref[...].T
    embedded = jnp.zeros(feats_ref.shape, jnp.float32)
    for kind in range(kinds):
        embedded = jnp.where(species_ref[...] == kind, columns[:held, kind : kind + 1], embedded)
    out_ref[0:held, :] = feats_ref[...] * embedded
    out_ref[held : held + count, 0:held] = radial_ref[...]
    out_ref[held + count : held + count + kinds, 0:held] = center_ref[...]
    for axis, length in enumerate((box_x, cross_width, cross_width)):
        own_ref[axis : axis + 1, :] = pos_ref[axis : axis + 1, :] * (1.0 / length)
    own_ref[3:4, :] = species_ref[...].astype(jnp.float32)


def pack(box_x, node_features, species, positions, species_embed, radial_weight, center_embed):
    held, atoms = node_features.shape
    operands = (
        node_features,
        species[None],
        positions,
        species_embed.T,
        radial_weight,
        center_embed.T,
    )
    operands = [pltpu.with_memory_space_constraint(x, pltpu.HBM) for x in operands]
    return pl.pallas_call(
        functools.partial(pack_kernel, box_x),
        out_shape=(
            jax.ShapeDtypeStruct((held + tile, atoms), jnp.float32),
            jax.ShapeDtypeStruct((8, atoms), jnp.float32),
        ),
        in_specs=[pl.BlockSpec(memory_space=pltpu.HBM)] * len(operands),
        out_specs=[pl.BlockSpec(memory_space=pltpu.VMEM)] * 2,
        scratch_shapes=[pltpu.VMEM(x.shape, x.dtype) for x in operands]
        + [pltpu.VMEM((8, lanes), jnp.float32), pltpu.SemaphoreType.DMA((len(operands),))],
        compiler_params=pltpu.CompilerParams(vmem_limit_bytes=1 << 20),
        name="pack",
    )(*operands)


def moved(value, axis, target):
    size = lax.axis_size(axis)
    return lax.ppermute(value, axis, [(i, target(i, size)) for i in range(size)])


def flipped(value, axis, bit):
    return moved(value, axis, lambda i, size: i ^ bit)


def shards(
    positions,
    species,
    node_features,
    block_mask,
    radial_weight,
    species_embed,
    center_embed,
    mix_weight,
):
    slab_count = lax.axis_size("blk")
    owner_count = lax.axis_size("chan")
    box_x = float(slab_count) * slab_width
    reach = (block_mask.shape[1] - 1) // 2
    count = radial_weight.shape[0]
    kinds = species_embed.shape[1]
    held, atoms = node_features.shape
    me = lax.axis_index("blk")
    owner = lax.axis_index("chan")

    owned, pos = pack(
        box_x, node_features, species, positions, species_embed, radial_weight, center_embed
    )
    owned = owned[None]
    bit = owner_count // 2
    flips = [0]
    while bit:
        owned = jnp.concatenate([owned, flipped(owned, "chan", bit)], axis=0)
        flips = flips + [f ^ bit for f in flips]
        bit //= 2
    channels = held * owner_count
    feats = owned[:, :held].reshape(channels, atoms)
    par = owned[:, held : held + count + kinds, :held].transpose(0, 2, 1)
    par = par.reshape(channels, count + kinds)
    mine = lax.dynamic_slice_in_dim(mix_weight, owner * held, held, 1)
    mix = jnp.concatenate(
        [lax.dynamic_slice_in_dim(mine, (owner ^ f) * held, held, 2) for f in flips], axis=2
    )

    bundle = jnp.concatenate([feats, pos], axis=0)
    depth = bundle.shape[0]

    def activity(places):
        offset = jnp.stack([lax.rem(p - me + reach + slab_count, slab_count) for p in places])
        at = offset[:, None] == jnp.arange(2 * reach + 1, dtype=jnp.int32)[None, :]
        value = jnp.sum(jnp.where(at, block_mask, 0), axis=1).astype(jnp.float32)
        return jnp.broadcast_to(value[:, None], (len(places), atoms))

    call = lambda act, data, slabs, start, mix=None: accumulate(
        pos, act, data, slabs, 0, box_x, count, start, mix
    )
    if slab_count == 2 * (reach + 1) == 8:
        act = activity([me ^ j for j in range(slab_count)])
        three = flipped(bundle, "blk", 3)
        acc = call(act, [bundle], [(0, 0, 0)], par)
        three, acc = lax.optimization_barrier((three, acc))
        pair = jnp.concatenate([bundle, three], axis=0)
        five = flipped(pair, "blk", 5)
        one = flipped(pair, "blk", 1)
        acc = call(act, [three], [(0, 0, 3)], acc)
        acc = call(act, [one], [(0, 0, 1), (0, depth, 2)], acc)
        five, acc = lax.optimization_barrier((five, acc))
        seven = flipped(five[depth:], "blk", 1)
        acc = call(act, [five], [(0, 0, 5)], acc)
        seven, acc = lax.optimization_barrier((seven, acc))
        return call(act, [five, seven], [(0, depth, 6), (1, 0, 7)], acc, mix)
    places = [0] + [k for h in range(1, reach + 1) for k in (h, -h)]
    act = activity([lax.rem(me + k + slab_count, slab_count) for k in places])
    act = jnp.pad(act, ((0, 8 - len(places)), (0, 0)))
    data = [bundle] + [
        moved(bundle, "blk", lambda i, size, k=k: (i - k) % size) for k in places[1:]
    ]
    return call(act, data, [(j, 0, j) for j in range(len(places))], par, mix)


def solution(mesh):
    return jax.shard_map(
        shards,
        mesh=mesh,
        in_specs=(
            P(None, "blk"),
            P("blk"),
            P("chan", "blk"),
            P("blk", None),
            P(None, "chan"),
            P("chan", None),
            P("chan", None),
            P(),
        ),
        out_specs=P(None, "chan", "blk"),
        check_vma=False,
    )
```

```python
import functools
import math

import jax
import jax.numpy as jnp
from jax import lax
from jax.experimental import pallas as pl
from jax.experimental.pallas import tpu as pltpu
from jax.sharding import PartitionSpec as P


slab_width = 5.0 / 3.0
cross_width = 48.0
cut_radius = 5.0
soften = 0.25
components = 9
orders = ((0, 1), (1, 4), (4, 9))
lanes = 128
tile = 16

twice_cos_terms = (
    1.9999999781180455,
    -9.869602249726915,
    8.117389682486351,
    -2.670316860337427,
    0.4700596167989333,
    -0.05071796727719481,
    0.003187821366091919,
)
factors = (1.0, math.sqrt(3.0), math.sqrt(15.0))


def horner(terms, v):
    value = jnp.full_like(v, terms[-1])
    for term in terms[-2::-1]:
        value = value * v + term
    return value


def pair_rows(own, other, lengths, count, apart):
    shift = []
    for axis, length in enumerate(lengths):
        r = other[axis] - own[axis]
        shift.append(length * (r - jnp.round(r)))
    x, y, z = shift
    s = x * x + y * y + z * z + soften
    inverse = lax.rsqrt(s)
    square = s * (1.0 / cut_radius**2)
    sixth = square * square * square
    level = 0.5 * math.sqrt(2.0 / cut_radius)
    envelope = level + sixth * (
        square * (inverse * (48.0 * cut_radius * level) - 21.0 * level) - 28.0 * level
    )
    keep = square < 1.0
    if apart is not None:
        keep = jnp.logical_and(keep, apart)
    twice = horner(twice_cos_terms, square)
    rest = jnp.maximum(4.0 - twice * twice, 1e-12)
    sine = rest * lax.rsqrt(rest)
    first = jnp.where(keep, envelope, 0.0) * (sine * inverse)
    radial = [first, twice * first]
    while len(radial) < count:
        radial.append(twice * radial[-1] - radial[-2])
    x, y, z = x * inverse, y * inverse, z * inverse
    xx, yy = x * x, y * y
    harmonics = [
        None,
        x,
        y,
        z,
        x * y,
        y * z,
        z * z * (1.0 / math.sqrt(3.0)) - (xx + yy) * (0.5 / math.sqrt(3.0)),
        x * z,
        (xx - yy) * 0.5,
    ]
    radial = [r.astype(jnp.bfloat16) for r in radial[:count]]
    harmonics = [None if h is None else h.astype(jnp.bfloat16) for h in harmonics]
    return [[r if h is None else r * h for h in harmonics] for r in radial]


def pair_kernel(slabs, data_count, own_slab, first, last, box_x, count, *refs):
    refs = list(refs)
    pos_ref, act_ref = refs[:2]
    data = refs[2 : 2 + data_count]
    rest = refs[2 + data_count :]
    lengths = (box_x, cross_width, cross_width)
    own = [jnp.broadcast_to(pos_ref[axis : axis + 1, :], (tile, lanes)) for axis in range(3)]
    channels = rest[0].shape[0]
    lane = lax.broadcasted_iota(jnp.int32, (channels, lanes), 1)
    group, within = lane // tile, lax.rem(lane, tile)
    if first:
        par_ref = rest.pop(0)
        spread = jnp.broadcast_to(par_ref[:, 0:1], (channels, lanes))
        for n in range(1, count):
            spread = jnp.where(group == n, par_ref[:, n : n + 1], spread)
        centre = jnp.zeros((channels, lanes), jnp.float32)
        for kind in range(par_ref.shape[1] - count):
            here = pos_ref[3:4, :] == float(kind)
            centre = jnp.where(here, par_ref[:, count + kind : count + kind + 1], centre)
    else:
        acc_ref, spread_ref, centre_ref = rest.pop(0), rest.pop(0), rest.pop(0)
        spread = spread_ref[...]
    if last:
        mix_ref, out_ref, sum_ref = rest
    elif first:
        sum_ref, spread_ref, centre_ref = rest
        spread_ref[...] = spread
        centre_ref[...] = centre
    else:
        (sum_ref,) = rest
    part = None
    for pieces, (where, base), index in slabs:
        feats = [data[which][at : at + channels // len(pieces), :] for which, at in pieces]
        feats = feats[0] if len(feats) == 1 else jnp.concatenate(feats, axis=0)
        feats = feats * act_ref[index : index + 1, :]
        columns = data[where][base : base + 8, :].T
        for pair in range(lanes // (2 * tile)):
            weights, tables = [], []
            for step in (2 * pair, 2 * pair + 1):
                picked = jnp.take_along_axis(feats, within + step * tile, axis=1)
                weights.append((spread * picked).astype(jnp.bfloat16))
                rows = slice(step * tile, (step + 1) * tile)
                other = [
                    jnp.broadcast_to(columns[rows, axis : axis + 1], (tile, lanes))
                    for axis in range(3)
                ]
                apart = None
                if index == own_slab:
                    apart = (
                        lax.broadcasted_iota(jnp.int32, (tile, lanes), 0) + step * tile
                    ) != lax.broadcasted_iota(jnp.int32, (tile, lanes), 1)
                tables += pair_rows(own, other, lengths, count, apart)
            stacked = jnp.concatenate([jnp.concatenate(row, axis=1) for row in tables], axis=0)
            product = jnp.dot(
                jnp.concatenate(weights, axis=1), stacked, preferred_element_type=jnp.float32
            )
            part = product if part is None else part + product
    sum_ref[...] = part if first else acc_ref[...] + part
    if not last:
        return
    if not first:
        centre = centre_ref[...]
    held = mix_ref.shape[1]
    for order, (start, stop) in enumerate(orders):
        mix = mix_ref[order] * factors[order]
        mix_high = mix.astype(jnp.bfloat16)
        mix_low = (mix - mix_high.astype(jnp.float32)).astype(jnp.bfloat16)
        features = [sum_ref[:, m * lanes : (m + 1) * lanes] * centre for m in range(start, stop)]
        features = features[0] if len(features) == 1 else jnp.concatenate(features, axis=1)
        high = features.astype(jnp.bfloat16)
        low = (features - high.astype(jnp.float32)).astype(jnp.bfloat16)
        both = jnp.dot(
            jnp.concatenate([mix_high, mix_low], axis=0), high, preferred_element_type=jnp.float32
        )
        mixed = both[:held] + both[held:]
        mixed = mixed + jnp.dot(mix_high, low, preferred_element_type=jnp.float32)
        total = None
        for m in range(stop - start):
            one = mixed[:, m * lanes : (m + 1) * lanes]
            total = one * one if total is None else total + one * one
        out_ref[order] = jnp.log1p(total)


def accumulate(pos, act, data, slabs, own_slab, box_x, count, start, mix=None):
    atoms = pos.shape[1]
    first, last = not isinstance(start, tuple), mix is not None
    channels = (start if first else start[1]).shape[0]
    operands = [pos, act, *data, *((start,) if first else start)]
    wide = jax.ShapeDtypeStruct((channels, components * atoms), jnp.float32)
    narrow = jax.ShapeDtypeStruct((channels, atoms), jnp.float32)
    if last:
        operands.append(mix)
        shapes = jax.ShapeDtypeStruct((len(orders), mix.shape[1], atoms), jnp.float32)
    else:
        shapes = [wide, narrow, narrow] if first else [wide]
    flops = 2 * channels * count * components * atoms * atoms * len(slabs)

    def body(*refs):
        pair_kernel(slabs, len(data), own_slab, first, last, box_x, count, *refs)

    whole = pl.BlockSpec(memory_space=pltpu.VMEM)
    result = pl.pallas_call(
        body,
        out_shape=shapes,
        in_specs=[whole] * len(operands),
        out_specs=whole if last else [whole] * len(shapes),
        scratch_shapes=[pltpu.VMEM(wide.shape, jnp.float32)] if last else [],
        cost_estimate=pl.CostEstimate(flops=flops, bytes_accessed=1 << 20, transcendentals=0),
        compiler_params=pltpu.CompilerParams(vmem_limit_bytes=16 << 20),
    )(*operands)
    return result if last else tuple(result) if first else (result[0], *start[1:])


def pack_kernel(box_x, *refs):
    sources, (out_ref, own_ref), held_refs = refs[:6], refs[6:8], refs[8:14]
    tile_ref, sems = refs[14:]
    copies = [
        pltpu.make_async_copy(source, held_ref, sems.at[i])
        for i, (source, held_ref) in enumerate(zip(sources, held_refs))
    ]
    for copy in copies:
        copy.start()
    feats_ref, species_ref, pos_ref, embed_ref, radial_ref, center_ref = held_refs
    held = feats_ref.shape[0]
    kinds, count = embed_ref.shape[0], radial_ref.shape[0]
    tile_ref[...] = jnp.zeros_like(tile_ref)
    out_ref[held:, :] = jnp.zeros((tile, lanes), jnp.float32)
    own_ref[...] = jnp.zeros_like(own_ref)
    for copy in copies:
        copy.wait()
    tile_ref[0:kinds, 0:held] = embed_ref[...]
    columns = tile_ref[...].T
    embedded = jnp.zeros(feats_ref.shape, jnp.float32)
    for kind in range(kinds):
        embedded = jnp.where(species_ref[...] == kind, columns[:held, kind : kind + 1], embedded)
    out_ref[0:held, :] = feats_ref[...] * embedded
    out_ref[held : held + count, 0:held] = radial_ref[...]
    out_ref[held + count : held + count + kinds, 0:held] = center_ref[...]
    for axis, length in enumerate((box_x, cross_width, cross_width)):
        own_ref[axis : axis + 1, :] = pos_ref[axis : axis + 1, :] * (1.0 / length)
    own_ref[3:4, :] = species_ref[...].astype(jnp.float32)


def pack(box_x, node_features, species, positions, species_embed, radial_weight, center_embed):
    held, atoms = node_features.shape
    operands = (
        node_features,
        species[None],
        positions,
        species_embed.T,
        radial_weight,
        center_embed.T,
    )
    operands = [pltpu.with_memory_space_constraint(x, pltpu.HBM) for x in operands]
    return pl.pallas_call(
        functools.partial(pack_kernel, box_x),
        out_shape=(
            jax.ShapeDtypeStruct((held + tile, atoms), jnp.float32),
            jax.ShapeDtypeStruct((8, atoms), jnp.float32),
        ),
        in_specs=[pl.BlockSpec(memory_space=pltpu.HBM)] * len(operands),
        out_specs=[pl.BlockSpec(memory_space=pltpu.VMEM)] * 2,
        scratch_shapes=[pltpu.VMEM(x.shape, x.dtype) for x in operands]
        + [pltpu.VMEM((8, lanes), jnp.float32), pltpu.SemaphoreType.DMA((len(operands),))],
        compiler_params=pltpu.CompilerParams(vmem_limit_bytes=1 << 20),
        name="pack",
    )(*operands)


def moved(value, axis, target):
    size = lax.axis_size(axis)
    return lax.ppermute(value, axis, [(i, target(i, size)) for i in range(size)])


def flipped(value, axis, bit):
    return moved(value, axis, lambda i, size: i ^ bit)


def crossed(value, bit):
    blocks, owners = lax.axis_size("blk"), lax.axis_size("chan")
    pairs = [
        (b * owners + c, (b ^ 1) * owners + (c ^ bit)) for b in range(blocks) for c in range(owners)
    ]
    return lax.ppermute(value, ("blk", "chan"), pairs)


def shards(
    positions,
    species,
    node_features,
    block_mask,
    radial_weight,
    species_embed,
    center_embed,
    mix_weight,
):
    slab_count = lax.axis_size("blk")
    owner_count = lax.axis_size("chan")
    box_x = float(slab_count) * slab_width
    reach = (block_mask.shape[1] - 1) // 2
    count = radial_weight.shape[0]
    kinds = species_embed.shape[1]
    held, atoms = node_features.shape
    me = lax.axis_index("blk")
    owner = lax.axis_index("chan")

    owned, pos = pack(
        box_x, node_features, species, positions, species_embed, radial_weight, center_embed
    )
    channels = held * owner_count
    crossing = slab_count == 2 * (reach + 1) == 8 and owner_count == 4
    if crossing:
        far = crossed(owned, 2)
        both = crossed(jnp.concatenate([owned, far], axis=0), 1)
        size = owned.shape[0]
        blocks, flips = [owned, both[size:], far, both[:size]], [0, 3, 2, 1]
    else:
        blocks, flips, bit = [owned], [0], owner_count // 2
        while bit:
            blocks = blocks + [flipped(block, "chan", bit) for block in blocks]
            flips = flips + [f ^ bit for f in flips]
            bit //= 2
    bundle = jnp.concatenate([block[:held] for block in blocks] + [pos], axis=0)
    par = jnp.concatenate([block[held : held + count + kinds, :held].T for block in blocks], axis=0)
    mine = lax.dynamic_slice_in_dim(mix_weight, owner * held, held, 1)
    mix = jnp.concatenate(
        [lax.dynamic_slice_in_dim(mine, (owner ^ f) * held, held, 2) for f in flips], axis=2
    )

    def activity(places):
        offset = jnp.stack([lax.rem(p - me + reach + slab_count, slab_count) for p in places])
        at = offset[:, None] == jnp.arange(2 * reach + 1, dtype=jnp.int32)[None, :]
        value = jnp.sum(jnp.where(at, block_mask, 0), axis=1).astype(jnp.float32)
        return jnp.broadcast_to(value[:, None], (len(places), atoms))

    call = lambda act, data, slabs, start, mix=None: accumulate(
        pos, act, data, slabs, 0, box_x, count, start, mix
    )
    if crossing:
        act = activity([me ^ j for j in range(slab_count)])
        half = channels // 2
        mixed = lambda a, b, index: (((a, 0), (b, half)), (a, channels), index)
        three = flipped(bundle, "blk", 3)
        one = flipped(bundle, "blk", 1)
        acc = call(act, [bundle, one], [mixed(0, 1, 0)], par)
        three, one, acc = lax.optimization_barrier((three, one, acc))
        pair = jnp.concatenate([bundle[:half], one[half:channels], pos, three], axis=0)
        five = flipped(pair, "blk", 5)
        two = flipped(three, "blk", 1)
        acc = call(act, [one, bundle], [mixed(0, 1, 1)], acc)
        acc = call(act, [three, two], [mixed(0, 1, 3), mixed(1, 0, 2)], acc)
        five, acc = lax.optimization_barrier((five, acc))
        depth = bundle.shape[0]
        five, six = five[:depth], five[depth:]
        seven = flipped(six, "blk", 1)
        acc = call(act, [five], [mixed(0, 0, 5)], acc)
        seven, acc = lax.optimization_barrier((seven, acc))
        return call(act, [six, seven], [mixed(0, 1, 6), mixed(1, 0, 7)], acc, mix)
    places = [0] + [k for h in range(1, reach + 1) for k in (h, -h)]
    act = activity([lax.rem(me + k + slab_count, slab_count) for k in places])
    act = jnp.pad(act, ((0, 8 - len(places)), (0, 0)))
    data = [bundle] + [
        moved(bundle, "blk", lambda i, size, k=k: (i - k) % size) for k in places[1:]
    ]
    slabs = [(((j, 0),), (j, channels), j) for j in range(len(places))]
    return call(act, data, slabs, par, mix)


def solution(mesh):
    return jax.shard_map(
        shards,
        mesh=mesh,
        in_specs=(
            P(None, "blk"),
            P("blk"),
            P("chan", "blk"),
            P("blk", None),
            P(None, "chan"),
            P("chan", None),
            P("chan", None),
            P(),
        ),
        out_specs=P(None, "chan", "blk"),
        check_vma=False,
    )
```

```python
import functools
import math

import jax
import jax.numpy as jnp
from jax import lax
from jax.experimental import pallas as pl
from jax.experimental.pallas import tpu as pltpu
from jax.sharding import PartitionSpec as P


slab_width = 5.0 / 3.0
cross_width = 48.0
cut_radius = 5.0
soften = 0.25
components = 9
orders = ((0, 1), (1, 4), (4, 9))
lanes = 128
tile = 16

twice_cos_terms = (
    1.9999999781180455,
    -9.869602249726915,
    8.117389682486351,
    -2.670316860337427,
    0.4700596167989333,
    -0.05071796727719481,
    0.003187821366091919,
)
factors = (1.0, math.sqrt(3.0), math.sqrt(15.0))


def horner(terms, v):
    value = jnp.full_like(v, terms[-1])
    for term in terms[-2::-1]:
        value = value * v + term
    return value


def pair_rows(own, other, lengths, count, apart):
    shift = []
    for axis, length in enumerate(lengths):
        r = other[axis] - own[axis]
        shift.append(length * (r - jnp.round(r)))
    x, y, z = shift
    s = x * x + y * y + z * z + soften
    inverse = lax.rsqrt(s)
    square = s * (1.0 / cut_radius**2)
    sixth = square * square * square
    level = 0.5 * math.sqrt(2.0 / cut_radius)
    envelope = level + sixth * (
        square * (inverse * (48.0 * cut_radius * level) - 21.0 * level) - 28.0 * level
    )
    keep = square < 1.0
    if apart is not None:
        keep = jnp.logical_and(keep, apart)
    twice = horner(twice_cos_terms, square)
    rest = jnp.maximum(4.0 - twice * twice, 1e-12)
    sine = rest * lax.rsqrt(rest)
    first = jnp.where(keep, envelope, 0.0) * (sine * inverse)
    radial = [first, twice * first]
    while len(radial) < count:
        radial.append(twice * radial[-1] - radial[-2])
    x, y, z = x * inverse, y * inverse, z * inverse
    xx, yy = x * x, y * y
    harmonics = [
        None,
        x,
        y,
        z,
        x * y,
        y * z,
        z * z * (1.0 / math.sqrt(3.0)) - (xx + yy) * (0.5 / math.sqrt(3.0)),
        x * z,
        (xx - yy) * 0.5,
    ]
    radial = [r.astype(jnp.bfloat16) for r in radial[:count]]
    harmonics = [None if h is None else h.astype(jnp.bfloat16) for h in harmonics]
    return [[r if h is None else r * h for h in harmonics] for r in radial]


def pair_kernel(slabs, data_count, own_slab, first, last, box_x, count, *refs):
    refs = list(refs)
    pos_ref, act_ref = refs[:2]
    data = refs[2 : 2 + data_count]
    rest = refs[2 + data_count :]
    lengths = (box_x, cross_width, cross_width)
    own = [jnp.broadcast_to(pos_ref[axis : axis + 1, :], (tile, lanes)) for axis in range(3)]
    channels = rest[0].shape[0]
    within = lax.rem(lax.broadcasted_iota(jnp.int32, (channels, lanes), 1), tile)
    spread_ref, centre_ref = rest.pop(0), rest.pop(0)
    spread = spread_ref[...]
    if not first:
        acc_ref = rest.pop(0)
    if last:
        mix_ref, out_ref, sum_ref = rest
    else:
        (sum_ref,) = rest
    part = None
    for pieces, (where, base), index in slabs:
        feats = [data[which][at : at + channels // len(pieces), :] for which, at in pieces]
        feats = feats[0] if len(feats) == 1 else jnp.concatenate(feats, axis=0)
        feats = feats * act_ref[index : index + 1, 0:1]
        columns = data[where][base : base + 8, :].T
        for pair in range(lanes // (2 * tile)):
            weights, tables = [], []
            for step in (2 * pair, 2 * pair + 1):
                picked = jnp.take_along_axis(feats, within + step * tile, axis=1)
                weights.append((spread * picked).astype(jnp.bfloat16))
                rows = slice(step * tile, (step + 1) * tile)
                other = [
                    jnp.broadcast_to(columns[rows, axis : axis + 1], (tile, lanes))
                    for axis in range(3)
                ]
                apart = None
                if index == own_slab:
                    apart = (
                        lax.broadcasted_iota(jnp.int32, (tile, lanes), 0) + step * tile
                    ) != lax.broadcasted_iota(jnp.int32, (tile, lanes), 1)
                tables += pair_rows(own, other, lengths, count, apart)
            stacked = jnp.concatenate([jnp.concatenate(row, axis=1) for row in tables], axis=0)
            product = jnp.dot(
                jnp.concatenate(weights, axis=1), stacked, preferred_element_type=jnp.float32
            )
            part = product if part is None else part + product
    sum_ref[...] = part if first else acc_ref[...] + part
    if not last:
        return
    centre = centre_ref[...]
    held = mix_ref.shape[1]
    for order, (start, stop) in enumerate(orders):
        mix = mix_ref[order] * factors[order]
        mix_high = mix.astype(jnp.bfloat16)
        mix_low = (mix - mix_high.astype(jnp.float32)).astype(jnp.bfloat16)
        features = [sum_ref[:, m * lanes : (m + 1) * lanes] * centre for m in range(start, stop)]
        features = features[0] if len(features) == 1 else jnp.concatenate(features, axis=1)
        high = features.astype(jnp.bfloat16)
        low = (features - high.astype(jnp.float32)).astype(jnp.bfloat16)
        both = jnp.dot(
            jnp.concatenate([mix_high, mix_low], axis=0), high, preferred_element_type=jnp.float32
        )
        mixed = both[:held] + both[held:]
        mixed = mixed + jnp.dot(mix_high, low, preferred_element_type=jnp.float32)
        total = None
        for m in range(stop - start):
            one = mixed[:, m * lanes : (m + 1) * lanes]
            total = one * one if total is None else total + one * one
        out_ref[order] = jnp.log1p(total)


def spread_kernel(count, par_ref, pos_ref, spread_ref, centre_ref):
    group = lax.broadcasted_iota(jnp.int32, spread_ref.shape, 1) // tile
    spread = jnp.broadcast_to(par_ref[:, 0:1], spread_ref.shape)
    for n in range(1, count):
        spread = jnp.where(group == n, par_ref[:, n : n + 1], spread)
    spread_ref[...] = spread
    centre = jnp.zeros(centre_ref.shape, jnp.float32)
    for kind in range(par_ref.shape[1] - count):
        here = pos_ref[3:4, :] == float(kind)
        centre = jnp.where(here, par_ref[:, count + kind : count + kind + 1], centre)
    centre_ref[...] = centre


def spread_out(par, pos, count):
    whole = pl.BlockSpec(memory_space=pltpu.VMEM)
    narrow = jax.ShapeDtypeStruct((par.shape[0], pos.shape[1]), jnp.float32)
    return pl.pallas_call(
        functools.partial(spread_kernel, count),
        out_shape=[narrow, narrow],
        in_specs=[whole, whole],
        out_specs=[whole, whole],
        compiler_params=pltpu.CompilerParams(vmem_limit_bytes=1 << 20),
        name="spread",
    )(par, pos)


def accumulate(pos, act, data, slabs, own_slab, box_x, count, spread, acc=None, mix=None):
    channels, atoms = spread[0].shape
    first, last = acc is None, mix is not None
    operands = [pos, act, *data, *spread]
    wide = jax.ShapeDtypeStruct((channels, components * atoms), jnp.float32)
    shape, scratch = wide, []
    if not first:
        operands.append(acc)
    if last:
        operands.append(mix)
        shape = jax.ShapeDtypeStruct((len(orders), mix.shape[1], atoms), jnp.float32)
        scratch = [pltpu.VMEM(wide.shape, jnp.float32)]
    flops = 2 * channels * count * components * atoms * atoms * len(slabs)

    def body(*refs):
        pair_kernel(slabs, len(data), own_slab, first, last, box_x, count, *refs)

    whole = pl.BlockSpec(memory_space=pltpu.VMEM)
    return pl.pallas_call(
        body,
        out_shape=shape,
        in_specs=[whole] * len(operands),
        out_specs=whole,
        scratch_shapes=scratch,
        cost_estimate=pl.CostEstimate(flops=flops, bytes_accessed=1 << 20, transcendentals=0),
        compiler_params=pltpu.CompilerParams(vmem_limit_bytes=16 << 20),
    )(*operands)


def pack_kernel(box_x, *refs):
    sources, (out_ref, own_ref), held_refs = refs[:6], refs[6:8], refs[8:14]
    tile_ref, sems = refs[14:]
    copies = [
        pltpu.make_async_copy(source, held_ref, sems.at[i])
        for i, (source, held_ref) in enumerate(zip(sources, held_refs))
    ]
    for copy in copies:
        copy.start()
    feats_ref, species_ref, pos_ref, embed_ref, radial_ref, center_ref = held_refs
    held = feats_ref.shape[0]
    kinds, count = embed_ref.shape[0], radial_ref.shape[0]
    tile_ref[...] = jnp.zeros_like(tile_ref)
    out_ref[held:, :] = jnp.zeros((tile, lanes), jnp.float32)
    own_ref[...] = jnp.zeros_like(own_ref)
    for copy in copies:
        copy.wait()
    tile_ref[0:kinds, 0:held] = embed_ref[...]
    columns = tile_ref[...].T
    embedded = jnp.zeros(feats_ref.shape, jnp.float32)
    for kind in range(kinds):
        embedded = jnp.where(species_ref[...] == kind, columns[:held, kind : kind + 1], embedded)
    out_ref[0:held, :] = feats_ref[...] * embedded
    out_ref[held : held + count, 0:held] = radial_ref[...]
    out_ref[held + count : held + count + kinds, 0:held] = center_ref[...]
    for axis, length in enumerate((box_x, cross_width, cross_width)):
        own_ref[axis : axis + 1, :] = pos_ref[axis : axis + 1, :] * (1.0 / length)
    own_ref[3:4, :] = species_ref[...].astype(jnp.float32)


def pack(box_x, node_features, species, positions, species_embed, radial_weight, center_embed):
    held, atoms = node_features.shape
    operands = (
        node_features,
        species[None],
        positions,
        species_embed.T,
        radial_weight,
        center_embed.T,
    )
    operands = [pltpu.with_memory_space_constraint(x, pltpu.HBM) for x in operands]
    return pl.pallas_call(
        functools.partial(pack_kernel, box_x),
        out_shape=(
            jax.ShapeDtypeStruct((held + tile, atoms), jnp.float32),
            jax.ShapeDtypeStruct((8, atoms), jnp.float32),
        ),
        in_specs=[pl.BlockSpec(memory_space=pltpu.HBM)] * len(operands),
        out_specs=[pl.BlockSpec(memory_space=pltpu.VMEM)] * 2,
        scratch_shapes=[pltpu.VMEM(x.shape, x.dtype) for x in operands]
        + [pltpu.VMEM((8, lanes), jnp.float32), pltpu.SemaphoreType.DMA((len(operands),))],
        compiler_params=pltpu.CompilerParams(vmem_limit_bytes=1 << 20),
        name="pack",
    )(*operands)


def moved(value, axis, target):
    size = lax.axis_size(axis)
    return lax.ppermute(value, axis, [(i, target(i, size)) for i in range(size)])


def flipped(value, axis, bit):
    return moved(value, axis, lambda i, size: i ^ bit)


def crossed(value, bit):
    blocks, owners = lax.axis_size("blk"), lax.axis_size("chan")
    pairs = [
        (b * owners + c, (b ^ 1) * owners + (c ^ bit)) for b in range(blocks) for c in range(owners)
    ]
    return lax.ppermute(value, ("blk", "chan"), pairs)


def shards(
    positions,
    species,
    node_features,
    block_mask,
    radial_weight,
    species_embed,
    center_embed,
    mix_weight,
):
    slab_count = lax.axis_size("blk")
    owner_count = lax.axis_size("chan")
    box_x = float(slab_count) * slab_width
    reach = (block_mask.shape[1] - 1) // 2
    count = radial_weight.shape[0]
    kinds = species_embed.shape[1]
    held, _ = node_features.shape
    me = lax.axis_index("blk")
    owner = lax.axis_index("chan")

    owned, pos = pack(
        box_x, node_features, species, positions, species_embed, radial_weight, center_embed
    )
    channels = held * owner_count
    crossing = slab_count == 2 * (reach + 1) == 8 and owner_count == 4
    if crossing:
        far = crossed(owned, 2)
        both = crossed(jnp.concatenate([owned, far], axis=0), 1)
        size = owned.shape[0]
        blocks, flips = [owned, both[size:], far, both[:size]], [0, 3, 2, 1]
    else:
        blocks, flips, bit = [owned], [0], owner_count // 2
        while bit:
            blocks = blocks + [flipped(block, "chan", bit) for block in blocks]
            flips = flips + [f ^ bit for f in flips]
            bit //= 2
    bundle = jnp.concatenate([block[:held] for block in blocks] + [pos], axis=0)
    par = jnp.concatenate([block[held : held + count + kinds, :held].T for block in blocks], axis=0)
    mine = lax.dynamic_slice_in_dim(mix_weight, owner * held, held, 1)
    mix = jnp.concatenate(
        [lax.dynamic_slice_in_dim(mine, (owner ^ f) * held, held, 2) for f in flips], axis=2
    )

    def activity(places):
        offset = jnp.stack([lax.rem(p - me + reach + slab_count, slab_count) for p in places])
        at = offset[:, None] == jnp.arange(2 * reach + 1, dtype=jnp.int32)[None, :]
        value = jnp.sum(jnp.where(at, block_mask, 0), axis=1).astype(jnp.float32)
        return value[:, None]

    spread = spread_out(par, pos, count)
    call = lambda act, data, slabs, acc=None, mix=None: accumulate(
        pos, act, data, slabs, 0, box_x, count, spread, acc, mix
    )
    if crossing:
        act = activity([me ^ j for j in range(slab_count)])
        half = channels // 2
        mixed = lambda a, b, index: (((a, 0), (b, half)), (a, channels), index)
        three = flipped(bundle, "blk", 3)
        one = flipped(bundle, "blk", 1)
        acc = call(act, [bundle, one], [mixed(0, 1, 0)])
        three, one, acc = lax.optimization_barrier((three, one, acc))
        pair = jnp.concatenate([bundle[:half], one[half:channels], pos, three], axis=0)
        five = flipped(pair, "blk", 5)
        two = flipped(three, "blk", 1)
        acc = call(act, [one, bundle], [mixed(0, 1, 1)], acc)
        acc = call(act, [three, two], [mixed(0, 1, 3), mixed(1, 0, 2)], acc)
        five, acc = lax.optimization_barrier((five, acc))
        depth = bundle.shape[0]
        five, six = five[:depth], five[depth:]
        seven = flipped(six, "blk", 1)
        acc = call(act, [five], [mixed(0, 0, 5)], acc)
        seven, acc = lax.optimization_barrier((seven, acc))
        return call(act, [six, seven], [mixed(0, 1, 6), mixed(1, 0, 7)], acc, mix)
    places = [0] + [k for h in range(1, reach + 1) for k in (h, -h)]
    act = activity([lax.rem(me + k + slab_count, slab_count) for k in places])
    act = jnp.pad(act, ((0, 8 - len(places)), (0, 0)))
    data = [bundle] + [
        moved(bundle, "blk", lambda i, size, k=k: (i - k) % size) for k in places[1:]
    ]
    slabs = [(((j, 0),), (j, channels), j) for j in range(len(places))]
    return call(act, data, slabs, None, mix)


def solution(mesh):
    return jax.shard_map(
        shards,
        mesh=mesh,
        in_specs=(
            P(None, "blk"),
            P("blk"),
            P("chan", "blk"),
            P("blk", None),
            P(None, "chan"),
            P("chan", None),
            P("chan", None),
            P(),
        ),
        out_specs=P(None, "chan", "blk"),
        check_vma=False,
    )
```

```python
import functools
import math

import jax
import jax.numpy as jnp
from jax import lax
from jax.experimental import pallas as pl
from jax.experimental.pallas import tpu as pltpu
from jax.sharding import PartitionSpec as P


slab_width = 5.0 / 3.0
cross_width = 48.0
cut_radius = 5.0
soften = 0.25
components = 9
orders = ((0, 1), (1, 4), (4, 9))
lanes = 128
tile = 16

twice_cos_terms = (
    1.9999999781180455,
    -9.869602249726915,
    8.117389682486351,
    -2.670316860337427,
    0.4700596167989333,
    -0.05071796727719481,
    0.003187821366091919,
)
factors = (1.0, math.sqrt(3.0), math.sqrt(15.0))


def horner(terms, v):
    value = jnp.full_like(v, terms[-1])
    for term in terms[-2::-1]:
        value = value * v + term
    return value


def pair_rows(own, other, lengths, count, apart):
    shift = []
    for axis, length in enumerate(lengths):
        r = other[axis] - own[axis]
        shift.append(length * (r - jnp.round(r)))
    x, y, z = shift
    s = x * x + y * y + z * z + soften
    inverse = lax.rsqrt(s)
    square = s * (1.0 / cut_radius**2)
    sixth = square * square * square
    level = 0.5 * math.sqrt(2.0 / cut_radius)
    envelope = level + sixth * (
        square * (inverse * (48.0 * cut_radius * level) - 21.0 * level) - 28.0 * level
    )
    keep = square < 1.0
    if apart is not None:
        keep = jnp.logical_and(keep, apart)
    twice = horner(twice_cos_terms, square)
    rest = jnp.maximum(4.0 - twice * twice, 1e-12)
    sine = rest * lax.rsqrt(rest)
    first = jnp.where(keep, envelope, 0.0) * (sine * inverse)
    radial = [first, twice * first]
    while len(radial) < count:
        radial.append(twice * radial[-1] - radial[-2])
    x, y, z = x * inverse, y * inverse, z * inverse
    xx, yy = x * x, y * y
    harmonics = [
        None,
        x,
        y,
        z,
        x * y,
        y * z,
        z * z * (1.0 / math.sqrt(3.0)) - (xx + yy) * (0.5 / math.sqrt(3.0)),
        x * z,
        (xx - yy) * 0.5,
    ]
    radial = [r.astype(jnp.bfloat16) for r in radial[:count]]
    harmonics = [None if h is None else h.astype(jnp.bfloat16) for h in harmonics]
    return [[r if h is None else r * h for h in harmonics] for r in radial]


def pair_kernel(slabs, data_count, own_slab, first, last, box_x, count, *refs):
    refs = list(refs)
    pos_ref, act_ref = refs[:2]
    data = refs[2 : 2 + data_count]
    rest = refs[2 + data_count :]
    lengths = (box_x, cross_width, cross_width)
    own = [jnp.broadcast_to(pos_ref[axis : axis + 1, :], (tile, lanes)) for axis in range(3)]
    channels = rest[0].shape[0]
    within = lax.rem(lax.broadcasted_iota(jnp.int32, (channels, lanes), 1), tile)
    down = lax.broadcasted_iota(jnp.int32, (tile, lanes), 0)
    spread_ref, centre_ref = rest.pop(0), rest.pop(0)
    spread = spread_ref[...]
    if not first:
        acc_ref = rest.pop(0)
    if last:
        mix_ref, out_ref, sum_ref = rest
    else:
        (sum_ref,) = rest
    part = None
    for pieces, (where, base), index in slabs:
        feats = [data[which][at : at + channels // len(pieces), :] for which, at in pieces]
        feats = feats[0] if len(feats) == 1 else jnp.concatenate(feats, axis=0)
        feats = feats * act_ref[index : index + 1, 0:1]
        across = [
            jnp.broadcast_to(data[where][base + axis : base + axis + 1, :], (tile, lanes))
            for axis in range(3)
        ]
        for pair in range(lanes // (2 * tile)):
            weights, tables = [], []
            for step in (2 * pair, 2 * pair + 1):
                picked = jnp.take_along_axis(feats, within + step * tile, axis=1)
                weights.append((spread * picked).astype(jnp.bfloat16))
                other = [
                    jnp.take_along_axis(axis, down + step * tile, axis=1) for axis in across
                ]
                apart = None
                if index == own_slab:
                    apart = (
                        down + step * tile
                    ) != lax.broadcasted_iota(jnp.int32, (tile, lanes), 1)
                tables += pair_rows(own, other, lengths, count, apart)
            stacked = jnp.concatenate([jnp.concatenate(row, axis=1) for row in tables], axis=0)
            product = jnp.dot(
                jnp.concatenate(weights, axis=1), stacked, preferred_element_type=jnp.float32
            )
            part = product if part is None else part + product
    sum_ref[...] = part if first else acc_ref[...] + part
    if not last:
        return
    centre = centre_ref[...]
    held = mix_ref.shape[1]
    for order, (start, stop) in enumerate(orders):
        mix = mix_ref[order] * factors[order]
        mix_high = mix.astype(jnp.bfloat16)
        mix_low = (mix - mix_high.astype(jnp.float32)).astype(jnp.bfloat16)
        features = [sum_ref[:, m * lanes : (m + 1) * lanes] * centre for m in range(start, stop)]
        features = features[0] if len(features) == 1 else jnp.concatenate(features, axis=1)
        high = features.astype(jnp.bfloat16)
        low = (features - high.astype(jnp.float32)).astype(jnp.bfloat16)
        both = jnp.dot(
            jnp.concatenate([mix_high, mix_low], axis=0), high, preferred_element_type=jnp.float32
        )
        mixed = both[:held] + both[held:]
        mixed = mixed + jnp.dot(mix_high, low, preferred_element_type=jnp.float32)
        total = None
        for m in range(stop - start):
            one = mixed[:, m * lanes : (m + 1) * lanes]
            total = one * one if total is None else total + one * one
        out_ref[order] = jnp.log1p(total)


def spread_kernel(count, par_ref, pos_ref, spread_ref, centre_ref):
    group = lax.broadcasted_iota(jnp.int32, spread_ref.shape, 1) // tile
    spread = jnp.broadcast_to(par_ref[:, 0:1], spread_ref.shape)
    for n in range(1, count):
        spread = jnp.where(group == n, par_ref[:, n : n + 1], spread)
    spread_ref[...] = spread
    centre = jnp.zeros(centre_ref.shape, jnp.float32)
    for kind in range(par_ref.shape[1] - count):
        here = pos_ref[3:4, :] == float(kind)
        centre = jnp.where(here, par_ref[:, count + kind : count + kind + 1], centre)
    centre_ref[...] = centre


def spread_out(par, pos, count):
    whole = pl.BlockSpec(memory_space=pltpu.VMEM)
    narrow = jax.ShapeDtypeStruct((par.shape[0], pos.shape[1]), jnp.float32)
    return pl.pallas_call(
        functools.partial(spread_kernel, count),
        out_shape=[narrow, narrow],
        in_specs=[whole, whole],
        out_specs=[whole, whole],
        compiler_params=pltpu.CompilerParams(vmem_limit_bytes=1 << 20),
        name="spread",
    )(par, pos)


def accumulate(pos, act, data, slabs, own_slab, box_x, count, spread, acc=None, mix=None):
    channels, atoms = spread[0].shape
    first, last = acc is None, mix is not None
    operands = [pos, act, *data, *spread]
    wide = jax.ShapeDtypeStruct((channels, components * atoms), jnp.float32)
    shape, scratch = wide, []
    if not first:
        operands.append(acc)
    if last:
        operands.append(mix)
        shape = jax.ShapeDtypeStruct((len(orders), mix.shape[1], atoms), jnp.float32)
        scratch = [pltpu.VMEM(wide.shape, jnp.float32)]
    flops = 2 * channels * count * components * atoms * atoms * len(slabs)

    def body(*refs):
        pair_kernel(slabs, len(data), own_slab, first, last, box_x, count, *refs)

    whole = pl.BlockSpec(memory_space=pltpu.VMEM)
    return pl.pallas_call(
        body,
        out_shape=shape,
        in_specs=[whole] * len(operands),
        out_specs=whole,
        scratch_shapes=scratch,
        cost_estimate=pl.CostEstimate(flops=flops, bytes_accessed=1 << 20, transcendentals=0),
        compiler_params=pltpu.CompilerParams(vmem_limit_bytes=16 << 20),
    )(*operands)


def pack_kernel(box_x, *refs):
    sources, (out_ref, own_ref), held_refs = refs[:6], refs[6:8], refs[8:14]
    tile_ref, sems = refs[14:]
    copies = [
        pltpu.make_async_copy(source, held_ref, sems.at[i])
        for i, (source, held_ref) in enumerate(zip(sources, held_refs))
    ]
    for copy in copies:
        copy.start()
    feats_ref, species_ref, pos_ref, embed_ref, radial_ref, center_ref = held_refs
    held = feats_ref.shape[0]
    kinds, count = embed_ref.shape[0], radial_ref.shape[0]
    tile_ref[...] = jnp.zeros_like(tile_ref)
    out_ref[held:, :] = jnp.zeros((tile, lanes), jnp.float32)
    own_ref[...] = jnp.zeros_like(own_ref)
    for copy in copies:
        copy.wait()
    tile_ref[0:kinds, 0:held] = embed_ref[...]
    columns = tile_ref[...].T
    embedded = jnp.zeros(feats_ref.shape, jnp.float32)
    for kind in range(kinds):
        embedded = jnp.where(species_ref[...] == kind, columns[:held, kind : kind + 1], embedded)
    out_ref[0:held, :] = feats_ref[...] * embedded
    out_ref[held : held + count, 0:held] = radial_ref[...]
    out_ref[held + count : held + count + kinds, 0:held] = center_ref[...]
    for axis, length in enumerate((box_x, cross_width, cross_width)):
        own_ref[axis : axis + 1, :] = pos_ref[axis : axis + 1, :] * (1.0 / length)
    own_ref[3:4, :] = species_ref[...].astype(jnp.float32)


def pack(box_x, node_features, species, positions, species_embed, radial_weight, center_embed):
    held, atoms = node_features.shape
    operands = (
        node_features,
        species[None],
        positions,
        species_embed.T,
        radial_weight,
        center_embed.T,
    )
    operands = [pltpu.with_memory_space_constraint(x, pltpu.HBM) for x in operands]
    return pl.pallas_call(
        functools.partial(pack_kernel, box_x),
        out_shape=(
            jax.ShapeDtypeStruct((held + tile, atoms), jnp.float32),
            jax.ShapeDtypeStruct((8, atoms), jnp.float32),
        ),
        in_specs=[pl.BlockSpec(memory_space=pltpu.HBM)] * len(operands),
        out_specs=[pl.BlockSpec(memory_space=pltpu.VMEM)] * 2,
        scratch_shapes=[pltpu.VMEM(x.shape, x.dtype) for x in operands]
        + [pltpu.VMEM((8, lanes), jnp.float32), pltpu.SemaphoreType.DMA((len(operands),))],
        compiler_params=pltpu.CompilerParams(vmem_limit_bytes=1 << 20),
        name="pack",
    )(*operands)


def moved(value, axis, target):
    size = lax.axis_size(axis)
    return lax.ppermute(value, axis, [(i, target(i, size)) for i in range(size)])


def flipped(value, axis, bit):
    return moved(value, axis, lambda i, size: i ^ bit)


def crossed(value, bit):
    blocks, owners = lax.axis_size("blk"), lax.axis_size("chan")
    pairs = [
        (b * owners + c, (b ^ 1) * owners + (c ^ bit)) for b in range(blocks) for c in range(owners)
    ]
    return lax.ppermute(value, ("blk", "chan"), pairs)


def shards(
    positions,
    species,
    node_features,
    block_mask,
    radial_weight,
    species_embed,
    center_embed,
    mix_weight,
):
    slab_count = lax.axis_size("blk")
    owner_count = lax.axis_size("chan")
    box_x = float(slab_count) * slab_width
    reach = (block_mask.shape[1] - 1) // 2
    count = radial_weight.shape[0]
    kinds = species_embed.shape[1]
    held, _ = node_features.shape
    me = lax.axis_index("blk")
    owner = lax.axis_index("chan")

    owned, pos = pack(
        box_x, node_features, species, positions, species_embed, radial_weight, center_embed
    )
    channels = held * owner_count
    crossing = slab_count == 2 * (reach + 1) == 8 and owner_count == 4
    if crossing:
        far = crossed(owned, 2)
        both = crossed(jnp.concatenate([owned, far], axis=0), 1)
        size = owned.shape[0]
        blocks, flips = [owned, both[size:], far, both[:size]], [0, 3, 2, 1]
    else:
        blocks, flips, bit = [owned], [0], owner_count // 2
        while bit:
            blocks = blocks + [flipped(block, "chan", bit) for block in blocks]
            flips = flips + [f ^ bit for f in flips]
            bit //= 2
    bundle = jnp.concatenate([block[:held] for block in blocks] + [pos], axis=0)
    par = jnp.concatenate([block[held : held + count + kinds, :held].T for block in blocks], axis=0)
    mine = lax.dynamic_slice_in_dim(mix_weight, owner * held, held, 1)
    mix = jnp.concatenate(
        [lax.dynamic_slice_in_dim(mine, (owner ^ f) * held, held, 2) for f in flips], axis=2
    )

    def activity(places):
        offset = jnp.stack([lax.rem(p - me + reach + slab_count, slab_count) for p in places])
        at = offset[:, None] == jnp.arange(2 * reach + 1, dtype=jnp.int32)[None, :]
        value = jnp.sum(jnp.where(at, block_mask, 0), axis=1).astype(jnp.float32)
        return value[:, None]

    spread = spread_out(par, pos, count)
    call = lambda act, data, slabs, acc=None, mix=None: accumulate(
        pos, act, data, slabs, 0, box_x, count, spread, acc, mix
    )
    if crossing:
        act = activity([me ^ j for j in range(slab_count)])
        half = channels // 2
        mixed = lambda a, b, index: (((a, 0), (b, half)), (a, channels), index)
        three = flipped(bundle, "blk", 3)
        one = flipped(bundle, "blk", 1)
        acc = call(act, [bundle, one], [mixed(0, 1, 0)])
        three, one, acc = lax.optimization_barrier((three, one, acc))
        pair = jnp.concatenate([bundle[:half], one[half:channels], pos, three], axis=0)
        five = flipped(pair, "blk", 5)
        two = flipped(three, "blk", 1)
        acc = call(act, [one, bundle], [mixed(0, 1, 1)], acc)
        acc = call(act, [three, two], [mixed(0, 1, 3), mixed(1, 0, 2)], acc)
        five, acc = lax.optimization_barrier((five, acc))
        depth = bundle.shape[0]
        five, six = five[:depth], five[depth:]
        seven = flipped(six, "blk", 1)
        acc = call(act, [five], [mixed(0, 0, 5)], acc)
        seven, acc = lax.optimization_barrier((seven, acc))
        return call(act, [six, seven], [mixed(0, 1, 6), mixed(1, 0, 7)], acc, mix)
    places = [0] + [k for h in range(1, reach + 1) for k in (h, -h)]
    act = activity([lax.rem(me + k + slab_count, slab_count) for k in places])
    act = jnp.pad(act, ((0, 8 - len(places)), (0, 0)))
    data = [bundle] + [
        moved(bundle, "blk", lambda i, size, k=k: (i - k) % size) for k in places[1:]
    ]
    slabs = [(((j, 0),), (j, channels), j) for j in range(len(places))]
    return call(act, data, slabs, None, mix)


def solution(mesh):
    return jax.shard_map(
        shards,
        mesh=mesh,
        in_specs=(
            P(None, "blk"),
            P("blk"),
            P("chan", "blk"),
            P("blk", None),
            P(None, "chan"),
            P("chan", None),
            P("chan", None),
            P(),
        ),
        out_specs=P(None, "chan", "blk"),
        check_vma=False,
    )
```

```python
import functools
import math

import jax
import jax.numpy as jnp
from jax import lax
from jax.experimental import pallas as pl
from jax.experimental.pallas import tpu as pltpu
from jax.sharding import PartitionSpec as P


slab_width = 5.0 / 3.0
cross_width = 48.0
cut_radius = 5.0
soften = 0.25
components = 9
orders = ((0, 1), (1, 4), (4, 9))
lanes = 128
tile = 16

twice_cos_terms = (
    1.9999999781180455,
    -9.869602249726915,
    8.117389682486351,
    -2.670316860337427,
    0.4700596167989333,
    -0.05071796727719481,
    0.003187821366091919,
)
factors = (1.0, math.sqrt(3.0), math.sqrt(15.0))
own_factors = {6: 0.5 / math.sqrt(3.0), 8: 0.5}


def horner(terms, v):
    value = jnp.full_like(v, terms[-1])
    for term in terms[-2::-1]:
        value = value * v + term
    return value


def pair_rows(own, other, count, apart):
    x = other[0] - own[0]
    y, z = (r - jnp.round(r) for r in (other[1] - own[1], other[2] - own[2]))
    s = x * x + y * y + z * z + soften / cross_width**2
    inverse = lax.rsqrt(s)
    square = s * (cross_width / cut_radius) ** 2
    sixth = square * square * square
    level = 0.5 * math.sqrt(2.0 / cut_radius) / cross_width
    envelope = level + sixth * (
        square * (inverse * (48.0 * cut_radius / cross_width * level) - 21.0 * level)
        - 28.0 * level
    )
    envelope = jnp.maximum(envelope, 0.0)
    if apart is not None:
        envelope = jnp.where(apart, envelope, 0.0)
    twice = horner(twice_cos_terms, square)
    rest = jnp.maximum(4.0 - twice * twice, 1e-12)
    sine = rest * lax.rsqrt(rest)
    first = envelope * (sine * inverse)
    radial = [first, twice * first]
    while len(radial) < count:
        radial.append(twice * radial[-1] - radial[-2])
    x, y, z = x * inverse, y * inverse, z * inverse
    xx, yy, zz = x * x, y * y, z * z
    harmonics = [
        None,
        x,
        y,
        z,
        x * y,
        y * z,
        (zz + zz) - (xx + yy),
        x * z,
        xx - yy,
    ]
    radial = [r.astype(jnp.bfloat16) for r in radial[:count]]
    harmonics = [None if h is None else h.astype(jnp.bfloat16) for h in harmonics]
    return [[r if h is None else r * h for h in harmonics] for r in radial]


def pair_kernel(slabs, data_count, own_slab, first, last, count, *refs):
    refs = list(refs)
    pos_ref, act_ref = refs[:2]
    data = refs[2 : 2 + data_count]
    rest = refs[2 + data_count :]
    own = [jnp.broadcast_to(pos_ref[axis : axis + 1, :], (tile, lanes)) for axis in range(3)]
    channels = rest[0].shape[0]
    within = lax.rem(lax.broadcasted_iota(jnp.int32, (channels, lanes), 1), tile)
    down = lax.broadcasted_iota(jnp.int32, (tile, lanes), 0)
    spread_ref, centre_ref = rest.pop(0), rest.pop(0)
    spread = spread_ref[...]
    if not first:
        acc_ref = rest.pop(0)
    if last:
        mix_ref, out_ref, sum_ref = rest
    else:
        (sum_ref,) = rest
    part = None
    for pieces, (where, base), index in slabs:
        feats = [data[which][at : at + channels // len(pieces), :] for which, at in pieces]
        feats = feats[0] if len(feats) == 1 else jnp.concatenate(feats, axis=0)
        feats = feats * act_ref[index : index + 1, 0:1]
        across = [
            jnp.broadcast_to(data[where][base + axis : base + axis + 1, :], (tile, lanes))
            for axis in range(3)
        ]
        across[0] = across[0] + act_ref[index : index + 1, 1:2]
        for pair in range(lanes // (2 * tile)):
            weights, tables = [], []
            for step in (2 * pair, 2 * pair + 1):
                picked = jnp.take_along_axis(feats, within + step * tile, axis=1)
                weights.append((spread * picked).astype(jnp.bfloat16))
                other = [
                    jnp.take_along_axis(axis, down + step * tile, axis=1) for axis in across
                ]
                apart = None
                if index == own_slab:
                    apart = (
                        down + step * tile
                    ) != lax.broadcasted_iota(jnp.int32, (tile, lanes), 1)
                tables += pair_rows(own, other, count, apart)
            stacked = jnp.concatenate([jnp.concatenate(row, axis=1) for row in tables], axis=0)
            product = jnp.dot(
                jnp.concatenate(weights, axis=1), stacked, preferred_element_type=jnp.float32
            )
            part = product if part is None else part + product
    sum_ref[...] = part if first else acc_ref[...] + part
    if not last:
        return
    centre = centre_ref[...]
    held = mix_ref.shape[1]
    for order, (start, stop) in enumerate(orders):
        mix = mix_ref[order] * factors[order]
        mix_high = mix.astype(jnp.bfloat16)
        mix_low = (mix - mix_high.astype(jnp.float32)).astype(jnp.bfloat16)
        features = [
            sum_ref[:, m * lanes : (m + 1) * lanes] * (centre * own_factors.get(m, 1.0))
            for m in range(start, stop)
        ]
        features = features[0] if len(features) == 1 else jnp.concatenate(features, axis=1)
        high = features.astype(jnp.bfloat16)
        low = (features - high.astype(jnp.float32)).astype(jnp.bfloat16)
        both = jnp.dot(
            jnp.concatenate([mix_high, mix_low], axis=0), high, preferred_element_type=jnp.float32
        )
        mixed = both[:held] + both[held:]
        mixed = mixed + jnp.dot(mix_high, low, preferred_element_type=jnp.float32)
        total = None
        for m in range(stop - start):
            one = mixed[:, m * lanes : (m + 1) * lanes]
            total = one * one if total is None else total + one * one
        out_ref[order] = jnp.log1p(total)


def spread_kernel(count, par_ref, pos_ref, spread_ref, centre_ref):
    group = lax.broadcasted_iota(jnp.int32, spread_ref.shape, 1) // tile
    spread = jnp.broadcast_to(par_ref[:, 0:1], spread_ref.shape)
    for n in range(1, count):
        spread = jnp.where(group == n, par_ref[:, n : n + 1], spread)
    spread_ref[...] = spread
    centre = jnp.zeros(centre_ref.shape, jnp.float32)
    for kind in range(par_ref.shape[1] - count):
        here = pos_ref[3:4, :] == float(kind)
        centre = jnp.where(here, par_ref[:, count + kind : count + kind + 1], centre)
    centre_ref[...] = centre


def spread_out(par, pos, count):
    whole = pl.BlockSpec(memory_space=pltpu.VMEM)
    narrow = jax.ShapeDtypeStruct((par.shape[0], pos.shape[1]), jnp.float32)
    return pl.pallas_call(
        functools.partial(spread_kernel, count),
        out_shape=[narrow, narrow],
        in_specs=[whole, whole],
        out_specs=[whole, whole],
        compiler_params=pltpu.CompilerParams(vmem_limit_bytes=1 << 20),
        name="spread",
    )(par, pos)


def accumulate(pos, act, data, slabs, own_slab, count, spread, acc=None, mix=None):
    channels, atoms = spread[0].shape
    first, last = acc is None, mix is not None
    operands = [pos, act, *data, *spread]
    wide = jax.ShapeDtypeStruct((channels, components * atoms), jnp.float32)
    shape, scratch = wide, []
    if not first:
        operands.append(acc)
    if last:
        operands.append(mix)
        shape = jax.ShapeDtypeStruct((len(orders), mix.shape[1], atoms), jnp.float32)
        scratch = [pltpu.VMEM(wide.shape, jnp.float32)]
    flops = 2 * channels * count * components * atoms * atoms * len(slabs)

    def body(*refs):
        pair_kernel(slabs, len(data), own_slab, first, last, count, *refs)

    whole = pl.BlockSpec(memory_space=pltpu.VMEM)
    return pl.pallas_call(
        body,
        out_shape=shape,
        in_specs=[whole] * len(operands),
        out_specs=whole,
        scratch_shapes=scratch,
        cost_estimate=pl.CostEstimate(flops=flops, bytes_accessed=1 << 20, transcendentals=0),
        compiler_params=pltpu.CompilerParams(vmem_limit_bytes=16 << 20),
    )(*operands)


def pack_kernel(*refs):
    sources, (out_ref, own_ref), held_refs = refs[:6], refs[6:8], refs[8:14]
    tile_ref, sems = refs[14:]
    copies = [
        pltpu.make_async_copy(source, held_ref, sems.at[i])
        for i, (source, held_ref) in enumerate(zip(sources, held_refs))
    ]
    for copy in copies:
        copy.start()
    feats_ref, species_ref, pos_ref, embed_ref, radial_ref, center_ref = held_refs
    held = feats_ref.shape[0]
    kinds, count = embed_ref.shape[0], radial_ref.shape[0]
    tile_ref[...] = jnp.zeros_like(tile_ref)
    out_ref[held:, :] = jnp.zeros((count, lanes), jnp.float32)
    own_ref[...] = jnp.zeros_like(own_ref)
    for copy in copies:
        copy.wait()
    tile_ref[0:kinds, 0:held] = embed_ref[...]
    embedded = jnp.zeros(feats_ref.shape, jnp.float32)
    down = lax.broadcasted_iota(jnp.int32, feats_ref.shape, 0)
    for kind in range(kinds):
        across = jnp.broadcast_to(tile_ref[kind : kind + 1, :], feats_ref.shape)
        column = jnp.take_along_axis(across, down, axis=1)
        embedded = jnp.where(species_ref[...] == kind, column, embedded)
    out_ref[0:held, :] = feats_ref[...] * embedded
    out_ref[held : held + count, 0:held] = radial_ref[...]
    out_ref[held : held + kinds, held : 2 * held] = center_ref[...]
    own_ref[0:3, :] = pos_ref[...] * (1.0 / cross_width)
    own_ref[3:4, :] = species_ref[...].astype(jnp.float32)


def pack(node_features, species, positions, species_embed, radial_weight, center_embed):
    held, atoms = node_features.shape
    operands = (
        node_features,
        species[None],
        positions,
        species_embed.T,
        radial_weight,
        center_embed.T,
    )
    operands = [pltpu.with_memory_space_constraint(x, pltpu.HBM) for x in operands]
    return pl.pallas_call(
        pack_kernel,
        out_shape=(
            jax.ShapeDtypeStruct((held + radial_weight.shape[0], atoms), jnp.float32),
            jax.ShapeDtypeStruct((8, atoms), jnp.float32),
        ),
        in_specs=[pl.BlockSpec(memory_space=pltpu.HBM)] * len(operands),
        out_specs=[pl.BlockSpec(memory_space=pltpu.VMEM)] * 2,
        scratch_shapes=[pltpu.VMEM(x.shape, x.dtype) for x in operands]
        + [pltpu.VMEM((8, lanes), jnp.float32), pltpu.SemaphoreType.DMA((len(operands),))],
        compiler_params=pltpu.CompilerParams(vmem_limit_bytes=1 << 20),
        name="pack",
    )(*operands)


def moved(value, axis, target):
    size = lax.axis_size(axis)
    return lax.ppermute(value, axis, [(i, target(i, size)) for i in range(size)])


def flipped(value, axis, bit):
    return moved(value, axis, lambda i, size: i ^ bit)


def crossed(value, bit):
    blocks, owners = lax.axis_size("blk"), lax.axis_size("chan")
    pairs = [
        (b * owners + c, (b ^ 1) * owners + (c ^ bit)) for b in range(blocks) for c in range(owners)
    ]
    return lax.ppermute(value, ("blk", "chan"), pairs)


def shards(
    positions,
    species,
    node_features,
    block_mask,
    radial_weight,
    species_embed,
    center_embed,
    mix_weight,
):
    slab_count = lax.axis_size("blk")
    owner_count = lax.axis_size("chan")
    reach = (block_mask.shape[1] - 1) // 2
    count = radial_weight.shape[0]
    kinds = species_embed.shape[1]
    held, _ = node_features.shape
    me = lax.axis_index("blk")
    owner = lax.axis_index("chan")

    owned, pos = pack(
        node_features, species, positions, species_embed, radial_weight, center_embed
    )
    channels = held * owner_count
    crossing = slab_count == 2 * (reach + 1) == 8 and owner_count == 4
    if crossing:
        far = crossed(owned, 2)
        both = crossed(jnp.concatenate([owned, far], axis=0), 1)
        size = owned.shape[0]
        blocks, flips = [owned, both[size:], far, both[:size]], [0, 3, 2, 1]
    else:
        blocks, flips, bit = [owned], [0], owner_count // 2
        while bit:
            blocks = blocks + [flipped(block, "chan", bit) for block in blocks]
            flips = flips + [f ^ bit for f in flips]
            bit //= 2
    bundle = jnp.concatenate([block[:held] for block in blocks] + [pos], axis=0)
    radial = [block[held : held + count, :held] for block in blocks]
    centres = [block[held : held + kinds, held : 2 * held] for block in blocks]
    par = jnp.concatenate(
        [jnp.concatenate(pair, axis=0).T for pair in zip(radial, centres)], axis=0
    )
    mine = lax.dynamic_slice_in_dim(mix_weight, owner * held, held, 1)
    mix = jnp.concatenate(
        [lax.dynamic_slice_in_dim(mine, (owner ^ f) * held, held, 2) for f in flips], axis=2
    )

    def activity(places):
        place = jnp.stack(places)
        offset = lax.rem(place - me + reach + slab_count, slab_count)
        at = offset[:, None] == jnp.arange(2 * reach + 1, dtype=jnp.int32)[None, :]
        value = jnp.sum(jnp.where(at, block_mask, 0), axis=1).astype(jnp.float32)
        moves = (offset - reach - (place - me)).astype(jnp.float32) * (slab_width / cross_width)
        return jnp.stack([value, moves], axis=1)

    spread = spread_out(par, pos, count)
    call = lambda act, data, slabs, acc=None, mix=None: accumulate(
        pos, act, data, slabs, 0, count, spread, acc, mix
    )
    if crossing:
        act = activity([me ^ j for j in range(slab_count)])
        half = channels // 2
        mixed = lambda a, b, index: (((a, 0), (b, half)), (a, channels), index)
        three = flipped(bundle, "blk", 3)
        one = flipped(bundle, "blk", 1)
        acc = call(act, [bundle, one], [mixed(0, 1, 0)])
        three, one, acc = lax.optimization_barrier((three, one, acc))
        pair = jnp.concatenate([bundle[:half], one[half:channels], pos, three], axis=0)
        five = flipped(pair, "blk", 5)
        two = flipped(three, "blk", 1)
        acc = call(act, [one, bundle], [mixed(0, 1, 1)], acc)
        acc = call(act, [three, two], [mixed(0, 1, 3), mixed(1, 0, 2)], acc)
        five, acc = lax.optimization_barrier((five, acc))
        depth = bundle.shape[0]
        five, six = five[:depth], five[depth:]
        seven = flipped(six, "blk", 1)
        acc = call(act, [five], [mixed(0, 0, 5)], acc)
        seven, acc = lax.optimization_barrier((seven, acc))
        return call(act, [six, seven], [mixed(0, 1, 6), mixed(1, 0, 7)], acc, mix)
    places = [0] + [k for h in range(1, reach + 1) for k in (h, -h)]
    act = activity([lax.rem(me + k + slab_count, slab_count) for k in places])
    act = jnp.pad(act, ((0, 8 - len(places)), (0, 0)))
    data = [bundle] + [
        moved(bundle, "blk", lambda i, size, k=k: (i - k) % size) for k in places[1:]
    ]
    slabs = [(((j, 0),), (j, channels), j) for j in range(len(places))]
    return call(act, data, slabs, None, mix)


def solution(mesh):
    return jax.shard_map(
        shards,
        mesh=mesh,
        in_specs=(
            P(None, "blk"),
            P("blk"),
            P("chan", "blk"),
            P("blk", None),
            P(None, "chan"),
            P("chan", None),
            P("chan", None),
            P(),
        ),
        out_specs=P(None, "chan", "blk"),
        check_vma=False,
    )
```

```python
import functools
import math

import jax
import jax.numpy as jnp
from jax import lax
from jax.experimental import pallas as pl
from jax.experimental.pallas import tpu as pltpu
from jax.sharding import PartitionSpec as P


slab_width = 5.0 / 3.0
cross_width = 48.0
cut_radius = 5.0
soften = 0.25
components = 9
orders = ((0, 1), (1, 4), (4, 9))
lanes = 128
tile = 16

twice_cos_terms = (
    1.9999999781180455,
    -9.869602249726915,
    8.117389682486351,
    -2.670316860337427,
    0.4700596167989333,
    -0.05071796727719481,
    0.003187821366091919,
)
factors = (1.0, math.sqrt(3.0), math.sqrt(15.0))


def horner(terms, v):
    value = jnp.full_like(v, terms[-1])
    for term in terms[-2::-1]:
        value = value * v + term
    return value


def pair_rows(own, other, lengths, count, apart):
    shift = []
    for axis, length in enumerate(lengths):
        r = other[axis] - own[axis]
        shift.append(length * (r - jnp.round(r)))
    x, y, z = shift
    s = x * x + y * y + z * z + soften
    inverse = lax.rsqrt(s)
    square = s * (1.0 / cut_radius**2)
    sixth = square * square * square
    level = 0.5 * math.sqrt(2.0 / cut_radius)
    envelope = level + sixth * (
        square * (inverse * (48.0 * cut_radius * level) - 21.0 * level) - 28.0 * level
    )
    keep = square < 1.0
    if apart is not None:
        keep = jnp.logical_and(keep, apart)
    twice = horner(twice_cos_terms, square)
    rest = jnp.maximum(4.0 - twice * twice, 1e-12)
    sine = rest * lax.rsqrt(rest)
    first = jnp.where(keep, envelope, 0.0) * (sine * inverse)
    radial = [first, twice * first]
    while len(radial) < count:
        radial.append(twice * radial[-1] - radial[-2])
    x, y, z = x * inverse, y * inverse, z * inverse
    xx, yy = x * x, y * y
    harmonics = [
        None,
        x,
        y,
        z,
        x * y,
        y * z,
        z * z * (1.0 / math.sqrt(3.0)) - (xx + yy) * (0.5 / math.sqrt(3.0)),
        x * z,
        (xx - yy) * 0.5,
    ]
    radial = [r.astype(jnp.bfloat16) for r in radial[:count]]
    harmonics = [None if h is None else h.astype(jnp.bfloat16) for h in harmonics]
    return [[r if h is None else r * h for h in harmonics] for r in radial]


def pair_kernel(slabs, data_count, own_slab, first, last, box_x, count, *refs):
    refs = list(refs)
    pos_ref, act_ref = refs[:2]
    data = refs[2 : 2 + data_count]
    rest = refs[2 + data_count :]
    lengths = (box_x, cross_width, cross_width)
    own = [jnp.broadcast_to(pos_ref[axis : axis + 1, :], (tile, lanes)) for axis in range(3)]
    channels = rest[0].shape[0]
    within = lax.rem(lax.broadcasted_iota(jnp.int32, (channels, lanes), 1), tile)
    down = lax.broadcasted_iota(jnp.int32, (tile, lanes), 0)
    spread_ref, centre_ref = rest.pop(0), rest.pop(0)
    spread = spread_ref[...]
    if not first:
        acc_ref = rest.pop(0)
    if last:
        mix_ref, out_ref, sum_ref = rest
    else:
        (sum_ref,) = rest
    part = None
    for pieces, (where, base), index in slabs:
        feats = [data[which][at : at + channels // len(pieces), :] for which, at in pieces]
        feats = feats[0] if len(feats) == 1 else jnp.concatenate(feats, axis=0)
        feats = feats * act_ref[index : index + 1, 0:1]
        across = [
            jnp.broadcast_to(data[where][base + axis : base + axis + 1, :], (tile, lanes))
            for axis in range(3)
        ]
        for pair in range(lanes // (2 * tile)):
            weights, tables = [], []
            for step in (2 * pair, 2 * pair + 1):
                picked = jnp.take_along_axis(feats, within + step * tile, axis=1)
                weights.append((spread * picked).astype(jnp.bfloat16))
                other = [
                    jnp.take_along_axis(axis, down + step * tile, axis=1) for axis in across
                ]
                apart = None
                if index == own_slab:
                    apart = (
                        down + step * tile
                    ) != lax.broadcasted_iota(jnp.int32, (tile, lanes), 1)
                tables += pair_rows(own, other, lengths, count, apart)
            stacked = jnp.concatenate([jnp.concatenate(row, axis=1) for row in tables], axis=0)
            product = jnp.dot(
                jnp.concatenate(weights, axis=1), stacked, preferred_element_type=jnp.float32
            )
            part = product if part is None else part + product
    sum_ref[...] = part if first else acc_ref[...] + part
    if not last:
        return
    centre = centre_ref[...]
    held = mix_ref.shape[1]
    for order, (start, stop) in enumerate(orders):
        mix = mix_ref[order] * factors[order]
        mix_high = mix.astype(jnp.bfloat16)
        mix_low = (mix - mix_high.astype(jnp.float32)).astype(jnp.bfloat16)
        features = [sum_ref[:, m * lanes : (m + 1) * lanes] * centre for m in range(start, stop)]
        features = features[0] if len(features) == 1 else jnp.concatenate(features, axis=1)
        high = features.astype(jnp.bfloat16)
        low = (features - high.astype(jnp.float32)).astype(jnp.bfloat16)
        both = jnp.dot(
            jnp.concatenate([mix_high, mix_low], axis=0), high, preferred_element_type=jnp.float32
        )
        mixed = both[:held] + both[held:]
        mixed = mixed + jnp.dot(mix_high, low, preferred_element_type=jnp.float32)
        total = None
        for m in range(stop - start):
            one = mixed[:, m * lanes : (m + 1) * lanes]
            total = one * one if total is None else total + one * one
        out_ref[order] = jnp.log1p(total)


def spread_kernel(count, par_ref, pos_ref, spread_ref, centre_ref):
    group = lax.broadcasted_iota(jnp.int32, spread_ref.shape, 1) // tile
    spread = jnp.broadcast_to(par_ref[:, 0:1], spread_ref.shape)
    for n in range(1, count):
        spread = jnp.where(group == n, par_ref[:, n : n + 1], spread)
    spread_ref[...] = spread
    centre = jnp.zeros(centre_ref.shape, jnp.float32)
    for kind in range(par_ref.shape[1] - count):
        here = pos_ref[3:4, :] == float(kind)
        centre = jnp.where(here, par_ref[:, count + kind : count + kind + 1], centre)
    centre_ref[...] = centre


def spread_out(par, pos, count):
    whole = pl.BlockSpec(memory_space=pltpu.VMEM)
    narrow = jax.ShapeDtypeStruct((par.shape[0], pos.shape[1]), jnp.float32)
    return pl.pallas_call(
        functools.partial(spread_kernel, count),
        out_shape=[narrow, narrow],
        in_specs=[whole, whole],
        out_specs=[whole, whole],
        compiler_params=pltpu.CompilerParams(vmem_limit_bytes=1 << 20),
        name="spread",
    )(par, pos)


def accumulate(pos, act, data, slabs, own_slab, box_x, count, spread, acc=None, mix=None):
    channels, atoms = spread[0].shape
    first, last = acc is None, mix is not None
    operands = [pos, act, *data, *spread]
    wide = jax.ShapeDtypeStruct((channels, components * atoms), jnp.float32)
    shape, scratch = wide, []
    if not first:
        operands.append(acc)
    if last:
        operands.append(mix)
        shape = jax.ShapeDtypeStruct((len(orders), mix.shape[1], atoms), jnp.float32)
        scratch = [pltpu.VMEM(wide.shape, jnp.float32)]
    flops = 2 * channels * count * components * atoms * atoms * len(slabs)

    def body(*refs):
        pair_kernel(slabs, len(data), own_slab, first, last, box_x, count, *refs)

    whole = pl.BlockSpec(memory_space=pltpu.VMEM)
    return pl.pallas_call(
        body,
        out_shape=shape,
        in_specs=[whole] * len(operands),
        out_specs=whole,
        scratch_shapes=scratch,
        cost_estimate=pl.CostEstimate(flops=flops, bytes_accessed=1 << 20, transcendentals=0),
        compiler_params=pltpu.CompilerParams(vmem_limit_bytes=16 << 20),
    )(*operands)


def pack_kernel(box_x, *refs):
    sources, (out_ref, own_ref), held_refs = refs[:6], refs[6:8], refs[8:14]
    tile_ref, sems = refs[14:]
    copies = [
        pltpu.make_async_copy(source, held_ref, sems.at[i])
        for i, (source, held_ref) in enumerate(zip(sources, held_refs))
    ]
    for copy in copies:
        copy.start()
    feats_ref, species_ref, pos_ref, embed_ref, radial_ref, center_ref = held_refs
    held = feats_ref.shape[0]
    kinds, count = embed_ref.shape[0], radial_ref.shape[0]
    tile_ref[...] = jnp.zeros_like(tile_ref)
    out_ref[held:, :] = jnp.zeros((count, lanes), jnp.float32)
    own_ref[...] = jnp.zeros_like(own_ref)
    for copy in copies:
        copy.wait()
    tile_ref[0:kinds, 0:held] = embed_ref[...]
    embedded = jnp.zeros(feats_ref.shape, jnp.float32)
    down = lax.broadcasted_iota(jnp.int32, feats_ref.shape, 0)
    for kind in range(kinds):
        across = jnp.broadcast_to(tile_ref[kind : kind + 1, :], feats_ref.shape)
        column = jnp.take_along_axis(across, down, axis=1)
        embedded = jnp.where(species_ref[...] == kind, column, embedded)
    out_ref[0:held, :] = feats_ref[...] * embedded
    out_ref[held : held + count, 0:held] = radial_ref[...]
    out_ref[held : held + kinds, held : 2 * held] = center_ref[...]
    for axis, length in enumerate((box_x, cross_width, cross_width)):
        own_ref[axis : axis + 1, :] = pos_ref[axis : axis + 1, :] * (1.0 / length)
    own_ref[3:4, :] = species_ref[...].astype(jnp.float32)


def pack(box_x, node_features, species, positions, species_embed, radial_weight, center_embed):
    held, atoms = node_features.shape
    operands = (
        node_features,
        species[None],
        positions,
        species_embed.T,
        radial_weight,
        center_embed.T,
    )
    operands = [pltpu.with_memory_space_constraint(x, pltpu.HBM) for x in operands]
    return pl.pallas_call(
        functools.partial(pack_kernel, box_x),
        out_shape=(
            jax.ShapeDtypeStruct((held + radial_weight.shape[0], atoms), jnp.float32),
            jax.ShapeDtypeStruct((8, atoms), jnp.float32),
        ),
        in_specs=[pl.BlockSpec(memory_space=pltpu.HBM)] * len(operands),
        out_specs=[pl.BlockSpec(memory_space=pltpu.VMEM)] * 2,
        scratch_shapes=[pltpu.VMEM(x.shape, x.dtype) for x in operands]
        + [pltpu.VMEM((8, lanes), jnp.float32), pltpu.SemaphoreType.DMA((len(operands),))],
        compiler_params=pltpu.CompilerParams(vmem_limit_bytes=1 << 20),
        name="pack",
    )(*operands)


def moved(value, axis, target):
    size = lax.axis_size(axis)
    return lax.ppermute(value, axis, [(i, target(i, size)) for i in range(size)])


def flipped(value, axis, bit):
    return moved(value, axis, lambda i, size: i ^ bit)


def crossed(value, bit):
    blocks, owners = lax.axis_size("blk"), lax.axis_size("chan")
    pairs = [
        (b * owners + c, (b ^ 1) * owners + (c ^ bit)) for b in range(blocks) for c in range(owners)
    ]
    return lax.ppermute(value, ("blk", "chan"), pairs)


def shards(
    positions,
    species,
    node_features,
    block_mask,
    radial_weight,
    species_embed,
    center_embed,
    mix_weight,
):
    slab_count = lax.axis_size("blk")
    owner_count = lax.axis_size("chan")
    box_x = float(slab_count) * slab_width
    reach = (block_mask.shape[1] - 1) // 2
    count = radial_weight.shape[0]
    kinds = species_embed.shape[1]
    held, _ = node_features.shape
    me = lax.axis_index("blk")
    owner = lax.axis_index("chan")

    owned, pos = pack(
        box_x, node_features, species, positions, species_embed, radial_weight, center_embed
    )
    channels = held * owner_count
    crossing = slab_count == 2 * (reach + 1) == 8 and owner_count == 4
    if crossing:
        far = crossed(owned, 2)
        both = crossed(jnp.concatenate([owned, far], axis=0), 1)
        size = owned.shape[0]
        blocks, flips = [owned, both[size:], far, both[:size]], [0, 3, 2, 1]
    else:
        blocks, flips, bit = [owned], [0], owner_count // 2
        while bit:
            blocks = blocks + [flipped(block, "chan", bit) for block in blocks]
            flips = flips + [f ^ bit for f in flips]
            bit //= 2
    bundle = jnp.concatenate([block[:held] for block in blocks] + [pos], axis=0)
    radial = [block[held : held + count, :held] for block in blocks]
    centres = [block[held : held + kinds, held : 2 * held] for block in blocks]
    par = jnp.concatenate(
        [jnp.concatenate(pair, axis=0).T for pair in zip(radial, centres)], axis=0
    )
    mine = lax.dynamic_slice_in_dim(mix_weight, owner * held, held, 1)
    mix = jnp.concatenate(
        [lax.dynamic_slice_in_dim(mine, (owner ^ f) * held, held, 2) for f in flips], axis=2
    )

    def activity(places):
        offset = jnp.stack([lax.rem(p - me + reach + slab_count, slab_count) for p in places])
        at = offset[:, None] == jnp.arange(2 * reach + 1, dtype=jnp.int32)[None, :]
        value = jnp.sum(jnp.where(at, block_mask, 0), axis=1).astype(jnp.float32)
        return value[:, None]

    spread = spread_out(par, pos, count)
    call = lambda act, data, slabs, acc=None, mix=None: accumulate(
        pos, act, data, slabs, 0, box_x, count, spread, acc, mix
    )
    if crossing:
        act = activity([me ^ j for j in range(slab_count)])
        half = channels // 2
        mixed = lambda a, b, index: (((a, 0), (b, half)), (a, channels), index)
        three = flipped(bundle, "blk", 3)
        one = flipped(bundle, "blk", 1)
        acc = call(act, [bundle, one], [mixed(0, 1, 0)])
        three, one, acc = lax.optimization_barrier((three, one, acc))
        pair = jnp.concatenate([bundle[:half], one[half:channels], pos, three], axis=0)
        five = flipped(pair, "blk", 5)
        two = flipped(three, "blk", 1)
        acc = call(act, [one, bundle], [mixed(0, 1, 1)], acc)
        acc = call(act, [three, two], [mixed(0, 1, 3), mixed(1, 0, 2)], acc)
        five, acc = lax.optimization_barrier((five, acc))
        depth = bundle.shape[0]
        five, six = five[:depth], five[depth:]
        seven = flipped(six, "blk", 1)
        acc = call(act, [five], [mixed(0, 0, 5)], acc)
        seven, acc = lax.optimization_barrier((seven, acc))
        return call(act, [six, seven], [mixed(0, 1, 6), mixed(1, 0, 7)], acc, mix)
    places = [0] + [k for h in range(1, reach + 1) for k in (h, -h)]
    act = activity([lax.rem(me + k + slab_count, slab_count) for k in places])
    act = jnp.pad(act, ((0, 8 - len(places)), (0, 0)))
    data = [bundle] + [
        moved(bundle, "blk", lambda i, size, k=k: (i - k) % size) for k in places[1:]
    ]
    slabs = [(((j, 0),), (j, channels), j) for j in range(len(places))]
    return call(act, data, slabs, None, mix)


def solution(mesh):
    return jax.shard_map(
        shards,
        mesh=mesh,
        in_specs=(
            P(None, "blk"),
            P("blk"),
            P("chan", "blk"),
            P("blk", None),
            P(None, "chan"),
            P("chan", None),
            P("chan", None),
            P(),
        ),
        out_specs=P(None, "chan", "blk"),
        check_vma=False,
    )
```

```python
import functools
import math

import jax
import jax.numpy as jnp
from jax import lax
from jax.experimental import pallas as pl
from jax.experimental.pallas import tpu as pltpu
from jax.sharding import PartitionSpec as P


slab_width = 5.0 / 3.0
cross_width = 48.0
cut_radius = 5.0
soften = 0.25
components = 9
orders = ((0, 1), (1, 4), (4, 9))
lanes = 128
tile = 16

twice_cos_terms = (
    1.9999999781180455,
    -9.869602249726915,
    8.117389682486351,
    -2.670316860337427,
    0.4700596167989333,
    -0.05071796727719481,
    0.003187821366091919,
)
factors = (1.0, math.sqrt(3.0), math.sqrt(15.0))


def horner(terms, v):
    value = jnp.full_like(v, terms[-1])
    for term in terms[-2::-1]:
        value = value * v + term
    return value


def pair_rows(own, other, lengths, count, apart):
    shift = []
    for axis, length in enumerate(lengths):
        r = other[axis] - own[axis]
        shift.append(length * (r - jnp.round(r)))
    x, y, z = shift
    s = x * x + y * y + z * z + soften
    inverse = lax.rsqrt(s)
    square = s * (1.0 / cut_radius**2)
    sixth = square * square * square
    level = 0.5 * math.sqrt(2.0 / cut_radius)
    envelope = level + sixth * (
        square * (inverse * (48.0 * cut_radius * level) - 21.0 * level) - 28.0 * level
    )
    envelope = jnp.maximum(envelope, 0.0)
    if apart is not None:
        envelope = jnp.where(apart, envelope, 0.0)
    twice = horner(twice_cos_terms, square)
    rest = jnp.maximum(4.0 - twice * twice, 1e-12)
    sine = rest * lax.rsqrt(rest)
    first = envelope * (sine * inverse)
    radial = [first, twice * first]
    while len(radial) < count:
        radial.append(twice * radial[-1] - radial[-2])
    x, y, z = x * inverse, y * inverse, z * inverse
    xx, yy = x * x, y * y
    harmonics = [
        None,
        x,
        y,
        z,
        x * y,
        y * z,
        z * z * (1.0 / math.sqrt(3.0)) - (xx + yy) * (0.5 / math.sqrt(3.0)),
        x * z,
        (xx - yy) * 0.5,
    ]
    radial = [r.astype(jnp.bfloat16) for r in radial[:count]]
    harmonics = [None if h is None else h.astype(jnp.bfloat16) for h in harmonics]
    return [[r if h is None else r * h for h in harmonics] for r in radial]


def pair_kernel(slabs, data_count, own_slab, first, last, box_x, count, *refs):
    refs = list(refs)
    pos_ref, act_ref = refs[:2]
    data = refs[2 : 2 + data_count]
    rest = refs[2 + data_count :]
    lengths = (box_x, cross_width, cross_width)
    own = [jnp.broadcast_to(pos_ref[axis : axis + 1, :], (tile, lanes)) for axis in range(3)]
    channels = rest[0].shape[0]
    within = lax.rem(lax.broadcasted_iota(jnp.int32, (channels, lanes), 1), tile)
    down = lax.broadcasted_iota(jnp.int32, (tile, lanes), 0)
    spread_ref, centre_ref = rest.pop(0), rest.pop(0)
    spread = spread_ref[...]
    if not first:
        acc_ref = rest.pop(0)
    if last:
        mix_ref, out_ref, sum_ref = rest
    else:
        (sum_ref,) = rest
    part = None
    for pieces, (where, base), index in slabs:
        feats = [data[which][at : at + channels // len(pieces), :] for which, at in pieces]
        feats = feats[0] if len(feats) == 1 else jnp.concatenate(feats, axis=0)
        feats = feats * act_ref[index : index + 1, 0:1]
        across = [
            jnp.broadcast_to(data[where][base + axis : base + axis + 1, :], (tile, lanes))
            for axis in range(3)
        ]
        for pair in range(lanes // (2 * tile)):
            weights, tables = [], []
            for step in (2 * pair, 2 * pair + 1):
                picked = jnp.take_along_axis(feats, within + step * tile, axis=1)
                weights.append((spread * picked).astype(jnp.bfloat16))
                other = [
                    jnp.take_along_axis(axis, down + step * tile, axis=1) for axis in across
                ]
                apart = None
                if index == own_slab:
                    apart = (
                        down + step * tile
                    ) != lax.broadcasted_iota(jnp.int32, (tile, lanes), 1)
                tables += pair_rows(own, other, lengths, count, apart)
            stacked = jnp.concatenate([jnp.concatenate(row, axis=1) for row in tables], axis=0)
            product = jnp.dot(
                jnp.concatenate(weights, axis=1), stacked, preferred_element_type=jnp.float32
            )
            part = product if part is None else part + product
    sum_ref[...] = part if first else acc_ref[...] + part
    if not last:
        return
    centre = centre_ref[...]
    held = mix_ref.shape[1]
    for order, (start, stop) in enumerate(orders):
        mix = mix_ref[order] * factors[order]
        mix_high = mix.astype(jnp.bfloat16)
        mix_low = (mix - mix_high.astype(jnp.float32)).astype(jnp.bfloat16)
        features = [sum_ref[:, m * lanes : (m + 1) * lanes] * centre for m in range(start, stop)]
        features = features[0] if len(features) == 1 else jnp.concatenate(features, axis=1)
        high = features.astype(jnp.bfloat16)
        low = (features - high.astype(jnp.float32)).astype(jnp.bfloat16)
        both = jnp.dot(
            jnp.concatenate([mix_high, mix_low], axis=0), high, preferred_element_type=jnp.float32
        )
        mixed = both[:held] + both[held:]
        mixed = mixed + jnp.dot(mix_high, low, preferred_element_type=jnp.float32)
        total = None
        for m in range(stop - start):
            one = mixed[:, m * lanes : (m + 1) * lanes]
            total = one * one if total is None else total + one * one
        out_ref[order] = jnp.log1p(total)


def spread_kernel(count, par_ref, pos_ref, spread_ref, centre_ref):
    group = lax.broadcasted_iota(jnp.int32, spread_ref.shape, 1) // tile
    spread = jnp.broadcast_to(par_ref[:, 0:1], spread_ref.shape)
    for n in range(1, count):
        spread = jnp.where(group == n, par_ref[:, n : n + 1], spread)
    spread_ref[...] = spread
    centre = jnp.zeros(centre_ref.shape, jnp.float32)
    for kind in range(par_ref.shape[1] - count):
        here = pos_ref[3:4, :] == float(kind)
        centre = jnp.where(here, par_ref[:, count + kind : count + kind + 1], centre)
    centre_ref[...] = centre


def spread_out(par, pos, count):
    whole = pl.BlockSpec(memory_space=pltpu.VMEM)
    narrow = jax.ShapeDtypeStruct((par.shape[0], pos.shape[1]), jnp.float32)
    return pl.pallas_call(
        functools.partial(spread_kernel, count),
        out_shape=[narrow, narrow],
        in_specs=[whole, whole],
        out_specs=[whole, whole],
        compiler_params=pltpu.CompilerParams(vmem_limit_bytes=1 << 20),
        name="spread",
    )(par, pos)


def accumulate(pos, act, data, slabs, own_slab, box_x, count, spread, acc=None, mix=None):
    channels, atoms = spread[0].shape
    first, last = acc is None, mix is not None
    operands = [pos, act, *data, *spread]
    wide = jax.ShapeDtypeStruct((channels, components * atoms), jnp.float32)
    shape, scratch = wide, []
    if not first:
        operands.append(acc)
    if last:
        operands.append(mix)
        shape = jax.ShapeDtypeStruct((len(orders), mix.shape[1], atoms), jnp.float32)
        scratch = [pltpu.VMEM(wide.shape, jnp.float32)]
    flops = 2 * channels * count * components * atoms * atoms * len(slabs)

    def body(*refs):
        pair_kernel(slabs, len(data), own_slab, first, last, box_x, count, *refs)

    whole = pl.BlockSpec(memory_space=pltpu.VMEM)
    return pl.pallas_call(
        body,
        out_shape=shape,
        in_specs=[whole] * len(operands),
        out_specs=whole,
        scratch_shapes=scratch,
        cost_estimate=pl.CostEstimate(flops=flops, bytes_accessed=1 << 20, transcendentals=0),
        compiler_params=pltpu.CompilerParams(vmem_limit_bytes=16 << 20),
    )(*operands)


def pack_kernel(box_x, *refs):
    sources, (out_ref, own_ref), held_refs = refs[:6], refs[6:8], refs[8:14]
    tile_ref, sems = refs[14:]
    copies = [
        pltpu.make_async_copy(source, held_ref, sems.at[i])
        for i, (source, held_ref) in enumerate(zip(sources, held_refs))
    ]
    for copy in copies:
        copy.start()
    feats_ref, species_ref, pos_ref, embed_ref, radial_ref, center_ref = held_refs
    held = feats_ref.shape[0]
    kinds, count = embed_ref.shape[0], radial_ref.shape[0]
    tile_ref[...] = jnp.zeros_like(tile_ref)
    out_ref[held:, :] = jnp.zeros((count, lanes), jnp.float32)
    own_ref[...] = jnp.zeros_like(own_ref)
    for copy in copies:
        copy.wait()
    tile_ref[0:kinds, 0:held] = embed_ref[...]
    embedded = jnp.zeros(feats_ref.shape, jnp.float32)
    down = lax.broadcasted_iota(jnp.int32, feats_ref.shape, 0)
    for kind in range(kinds):
        across = jnp.broadcast_to(tile_ref[kind : kind + 1, :], feats_ref.shape)
        column = jnp.take_along_axis(across, down, axis=1)
        embedded = jnp.where(species_ref[...] == kind, column, embedded)
    out_ref[0:held, :] = feats_ref[...] * embedded
    out_ref[held : held + count, 0:held] = radial_ref[...]
    out_ref[held : held + kinds, held : 2 * held] = center_ref[...]
    for axis, length in enumerate((box_x, cross_width, cross_width)):
        own_ref[axis : axis + 1, :] = pos_ref[axis : axis + 1, :] * (1.0 / length)
    own_ref[3:4, :] = species_ref[...].astype(jnp.float32)


def pack(box_x, node_features, species, positions, species_embed, radial_weight, center_embed):
    held, atoms = node_features.shape
    operands = (
        node_features,
        species[None],
        positions,
        species_embed.T,
        radial_weight,
        center_embed.T,
    )
    operands = [pltpu.with_memory_space_constraint(x, pltpu.HBM) for x in operands]
    return pl.pallas_call(
        functools.partial(pack_kernel, box_x),
        out_shape=(
            jax.ShapeDtypeStruct((held + radial_weight.shape[0], atoms), jnp.float32),
            jax.ShapeDtypeStruct((8, atoms), jnp.float32),
        ),
        in_specs=[pl.BlockSpec(memory_space=pltpu.HBM)] * len(operands),
        out_specs=[pl.BlockSpec(memory_space=pltpu.VMEM)] * 2,
        scratch_shapes=[pltpu.VMEM(x.shape, x.dtype) for x in operands]
        + [pltpu.VMEM((8, lanes), jnp.float32), pltpu.SemaphoreType.DMA((len(operands),))],
        compiler_params=pltpu.CompilerParams(vmem_limit_bytes=1 << 20),
        name="pack",
    )(*operands)


def moved(value, axis, target):
    size = lax.axis_size(axis)
    return lax.ppermute(value, axis, [(i, target(i, size)) for i in range(size)])


def flipped(value, axis, bit):
    return moved(value, axis, lambda i, size: i ^ bit)


def crossed(value, bit):
    blocks, owners = lax.axis_size("blk"), lax.axis_size("chan")
    pairs = [
        (b * owners + c, (b ^ 1) * owners + (c ^ bit)) for b in range(blocks) for c in range(owners)
    ]
    return lax.ppermute(value, ("blk", "chan"), pairs)


def shards(
    positions,
    species,
    node_features,
    block_mask,
    radial_weight,
    species_embed,
    center_embed,
    mix_weight,
):
    slab_count = lax.axis_size("blk")
    owner_count = lax.axis_size("chan")
    box_x = float(slab_count) * slab_width
    reach = (block_mask.shape[1] - 1) // 2
    count = radial_weight.shape[0]
    kinds = species_embed.shape[1]
    held, _ = node_features.shape
    me = lax.axis_index("blk")
    owner = lax.axis_index("chan")

    owned, pos = pack(
        box_x, node_features, species, positions, species_embed, radial_weight, center_embed
    )
    channels = held * owner_count
    crossing = slab_count == 2 * (reach + 1) == 8 and owner_count == 4
    if crossing:
        far = crossed(owned, 2)
        both = crossed(jnp.concatenate([owned, far], axis=0), 1)
        size = owned.shape[0]
        blocks, flips = [owned, both[size:], far, both[:size]], [0, 3, 2, 1]
    else:
        blocks, flips, bit = [owned], [0], owner_count // 2
        while bit:
            blocks = blocks + [flipped(block, "chan", bit) for block in blocks]
            flips = flips + [f ^ bit for f in flips]
            bit //= 2
    bundle = jnp.concatenate([block[:held] for block in blocks] + [pos], axis=0)
    radial = [block[held : held + count, :held] for block in blocks]
    centres = [block[held : held + kinds, held : 2 * held] for block in blocks]
    par = jnp.concatenate(
        [jnp.concatenate(pair, axis=0).T for pair in zip(radial, centres)], axis=0
    )
    mine = lax.dynamic_slice_in_dim(mix_weight, owner * held, held, 1)
    mix = jnp.concatenate(
        [lax.dynamic_slice_in_dim(mine, (owner ^ f) * held, held, 2) for f in flips], axis=2
    )

    def activity(places):
        offset = jnp.stack([lax.rem(p - me + reach + slab_count, slab_count) for p in places])
        at = offset[:, None] == jnp.arange(2 * reach + 1, dtype=jnp.int32)[None, :]
        value = jnp.sum(jnp.where(at, block_mask, 0), axis=1).astype(jnp.float32)
        return value[:, None]

    spread = spread_out(par, pos, count)
    call = lambda act, data, slabs, acc=None, mix=None: accumulate(
        pos, act, data, slabs, 0, box_x, count, spread, acc, mix
    )
    if crossing:
        act = activity([me ^ j for j in range(slab_count)])
        half = channels // 2
        mixed = lambda a, b, index: (((a, 0), (b, half)), (a, channels), index)
        three = flipped(bundle, "blk", 3)
        one = flipped(bundle, "blk", 1)
        acc = call(act, [bundle, one], [mixed(0, 1, 0)])
        three, one, acc = lax.optimization_barrier((three, one, acc))
        pair = jnp.concatenate([bundle[:half], one[half:channels], pos, three], axis=0)
        five = flipped(pair, "blk", 5)
        two = flipped(three, "blk", 1)
        acc = call(act, [one, bundle], [mixed(0, 1, 1)], acc)
        acc = call(act, [three, two], [mixed(0, 1, 3), mixed(1, 0, 2)], acc)
        five, acc = lax.optimization_barrier((five, acc))
        depth = bundle.shape[0]
        five, six = five[:depth], five[depth:]
        seven = flipped(six, "blk", 1)
        acc = call(act, [five], [mixed(0, 0, 5)], acc)
        seven, acc = lax.optimization_barrier((seven, acc))
        return call(act, [six, seven], [mixed(0, 1, 6), mixed(1, 0, 7)], acc, mix)
    places = [0] + [k for h in range(1, reach + 1) for k in (h, -h)]
    act = activity([lax.rem(me + k + slab_count, slab_count) for k in places])
    act = jnp.pad(act, ((0, 8 - len(places)), (0, 0)))
    data = [bundle] + [
        moved(bundle, "blk", lambda i, size, k=k: (i - k) % size) for k in places[1:]
    ]
    slabs = [(((j, 0),), (j, channels), j) for j in range(len(places))]
    return call(act, data, slabs, None, mix)


def solution(mesh):
    return jax.shard_map(
        shards,
        mesh=mesh,
        in_specs=(
            P(None, "blk"),
            P("blk"),
            P("chan", "blk"),
            P("blk", None),
            P(None, "chan"),
            P("chan", None),
            P("chan", None),
            P(),
        ),
        out_specs=P(None, "chan", "blk"),
        check_vma=False,
    )
```
